32 devices in a mesh: rollout: 2 (over y), frame: 2 (over core), seq: 8 (over z, x).
Axes of the slice: x: 2, y: 2, z: 4, core: 2. Of those that a mesh axis runs over, the one named last changes fastest.
Arguments:
- queries: bfloat16 [4, 4, 64, 2048], P(('rollout', 'frame'), None, 'seq'), parts along dimension 0, may hold values from -13 to 13
- keys: bfloat16 [4, 4, 64, 2048], P(('rollout', 'frame'), None, 'seq'), parts along dimension 0, may hold values from -13 to 13
- values: bfloat16 [4, 4, 64, 2048], P(('rollout', 'frame'), None, 'seq'), parts along dimension 0, may hold values from -6 to 6
- slot_of: int32 [4, 4], P('rollout'), parts along dimension 0, may hold values from 0 to 7, as said below
- level_of: int32 [4, 4], P('rollout'), parts along dimension 0, may hold values from 0 to 7
- gate_table: float32 [8, 2048], replicated, may hold values from 0.25 to 2
Outputs:
- attended: bfloat16 [4, 4, 64, 2048], P(('rollout', 'frame'), None, 'seq'), parts along dimension 0
The draws below stay inside these ranges and needn't reach their ends.
There are 2 independent parts, one for each index of `rollout`. The reference program is written for one: setup_inputs(seed, part) draws one part's arguments, and reference() takes and returns one part's arrays. A program takes and returns all parts, laid end to end along the dimension named above; an argument that names none is the same for every part. Nothing has to cross between parts.
Inputs may be any that keep to these rules, and one draw needn't show every extreme that they name: `slot_of`: each number 0 to 7 is the slot of exactly one frame.
All inputs are finite; a program needn't handle non-finite values.
Results may differ from the reference program's by a relative error of at most 0.0055.
Values may be sent and summed in bfloat16 or wider, within the bound.
A program may use at most 64 MiB of HBM per device.

```python
import math
import jax
import jax.numpy as jnp
from jax import lax

H = 16
HEAD = 128
HD = 2048
F = 8
F_LOC = 4
N_TOK = 64
LEVELS = 8
N_FRAME = 2


def draw_queries(key, part):
    drawn = jnp.clip(3.0 * jax.random.normal(jax.random.fold_in(key, 1), (F, N_TOK, HD), jnp.float32), -12.0, 12.0)
    return drawn.reshape(F // F_LOC, F_LOC, N_TOK, HD).astype(jnp.bfloat16)


def draw_keys(key, part):
    drawn = jnp.clip(jax.random.normal(jax.random.fold_in(key, 2), (F, N_TOK, HD), jnp.float32), -4.0, 4.0)
    return drawn.reshape(F // F_LOC, F_LOC, N_TOK, HD).astype(jnp.bfloat16)


def draw_slot_of(key, part):
    order = jax.random.permutation(jax.random.fold_in(key, 3), F)
    return order.astype(jnp.int32).reshape(F // F_LOC, F_LOC)


def with_ends(drawn, stream_key, smallest, largest):
    index_at = [jax.random.randint(jax.random.fold_in(stream_key, axis), (), 0, length) for axis, length in enumerate(drawn.shape)]
    widest = drawn.shape.index(max(drawn.shape))
    neighbour = index_at[:widest] + [(index_at[widest] + 1) % drawn.shape[widest]] + index_at[widest + 1:]
    return drawn.at[tuple(index_at)].set(smallest).at[tuple(neighbour)].set(largest)


def block_scale(own_key, shape, split, smallest, high):
    loudness, own = 1.0, jax.random.fold_in(own_key, 6)
    for position, blocks in split:
        heights = jnp.exp(jax.random.uniform(jax.random.fold_in(own, position), (blocks,), jnp.float32, smallest / len(split), high / len(split)))
        loudness = loudness * jnp.repeat(heights, shape[position] // blocks).reshape([-1 if axis == position else 1 for axis in range(len(shape))])
    return loudness


def bell_draw(key, dims, spread, bound, shards=(), kind=jnp.bfloat16):
    drawn = jax.random.normal(key, dims, jnp.float32) * spread
    if len(shards) > 0:
        drawn = block_scale(key, dims, shards, -0.22, 0.18) * drawn
    return jnp.clip(drawn, min=-bound, max=bound).astype(kind)


def setup_inputs(seed: int = 0, part: int = 0) -> dict:
    seeds = jax.random.split(jax.random.key(seed), 7)
    part_keys = jax.random.split(jax.random.fold_in(seeds[6], part), 7)
    queries = draw_queries(jax.random.fold_in(jax.random.fold_in(seeds[6], part), 71), part)
    keys = draw_keys(jax.random.fold_in(jax.random.fold_in(seeds[6], part), 71), part)
    values = bell_draw(part_keys[2], (N_FRAME, F_LOC, N_TOK, HD), 1.0, 6.0, ((0, 2), (2, 8)))
    slot_of = draw_slot_of(jax.random.fold_in(jax.random.fold_in(seeds[6], part), 71), part)
    level_of = with_ends(jax.random.randint(part_keys[4], (N_FRAME, F_LOC), 0, LEVELS), jax.random.fold_in(part_keys[4], 1), 0, LEVELS - 1).astype(jnp.int32)
    gate_table = jnp.clip(jax.random.uniform(seeds[5], (LEVELS, HD), jnp.float32, 0.25, 2.0), 0.25, 2.0)
    return dict(queries=queries, keys=keys, values=values, slot_of=slot_of, level_of=level_of, gate_table=gate_table)


def reference(queries, keys, values, slot_of, level_of, gate_table):
    frames = queries.shape[0] * queries.shape[1]
    tokens = queries.shape[2]
    query_heads = queries.reshape(frames, tokens, H, HEAD)
    key_heads = keys.reshape(frames * tokens, H, HEAD)
    value_heads = values.reshape(frames * tokens, H, HEAD)
    slot_flat = slot_of.reshape(frames)
    key_slot = jnp.repeat(slot_flat, tokens)
    score_scale = 1.0 / math.sqrt(HEAD)

    def one_head(head):
        key_rows = key_heads[:, head, :]
        value_rows = value_heads[:, head, :]

        def one_frame(frame):
            query_rows = query_heads[frame, :, head, :]
            scores = jnp.dot(query_rows, key_rows.T, preferred_element_type=jnp.float32) * score_scale
            visible = key_slot <= slot_flat[frame]
            scores = jnp.where(visible[None, :], scores, -jnp.inf)
            weights = jnp.exp(scores - lax.optimization_barrier(jnp.max(scores, axis=1, keepdims=True))).astype(jnp.bfloat16)
            total = lax.optimization_barrier(jnp.sum(weights.astype(jnp.float32), axis=1))
            mixed = jnp.dot(weights, value_rows, preferred_element_type=jnp.float32)
            return mixed / total[:, None]
        return lax.map(one_frame, jnp.arange(frames, dtype=jnp.int32))
    mixed = lax.map(one_head, jnp.arange(H, dtype=jnp.int32))
    mixed = jnp.transpose(mixed, (1, 2, 0, 3)).reshape(frames, tokens, H * HEAD)
    gates = gate_table[level_of.reshape(frames)]
    attended = (mixed * gates[:, None, :]).astype(jnp.bfloat16)
    return attended.reshape(queries.shape)
```

```python
import functools
import math

import jax
import jax.numpy as jnp
from jax import lax
from jax.experimental import pallas as pl
from jax.experimental.pallas import tpu as pltpu
from jax.sharding import PartitionSpec as P

HEAD = 128
MESH = pl.DeviceIdType.MESH
MASKED = -1e30


def kernel(
    plan,
    slot_hbm,
    level_hbm,
    q_ref,
    k_ref,
    v_ref,
    gate_ref,
    out_ref,
    slot_ref,
    noise_ref,
    q_stage,
    k_stage,
    v_stage,
    q_held,
    k_held,
    v_held,
    gate_held,
    bias,
    gates,
    answer,
    stage_sems,
    send_sems,
    key_sems,
    value_sems,
    piece_sems,
    out_sem,
    ready_sems,
):
    frames, seqs, heads, heads_per, copies, sources, tiers, pieces, fold = plan
    devices = frames * seqs
    width = seqs // tiers
    crowd = frames * width
    per_piece = sources // pieces
    _, local_frames, tokens, _ = q_ref.shape
    key_rows = devices * local_frames * tokens
    my_frame, my_seq = lax.axis_index("frame"), lax.axis_index("seq")
    me = my_frame * seqs + my_seq
    my_tier = lax.div(my_seq, width)
    my_index = my_frame * width + lax.rem(my_seq, width)
    owners = tiers - fold
    members = 2 if fold else 1
    served = [
        lax.rem(me + member * fold * width, devices) * heads_per // copies
        for member in range(members)
    ]
    first_source = lax.rem(me, copies) * sources
    my_block = lax.div(me, sources)

    def place(device):
        return {"frame": lax.div(device, seqs), "seq": lax.rem(device, seqs)}

    def columns(head, count):
        return pl.ds(pl.multiple_of(head * HEAD, HEAD), count * HEAD)

    def member_of(tier, index):
        return lax.div(index, width) * seqs + tier * width + lax.rem(index, width)

    piece_width = seqs // pieces
    if pieces > 1:
        my_piece = lax.div(my_seq, piece_width)
        my_slot = my_frame * piece_width + lax.rem(my_seq, piece_width)
    else:
        my_piece = 0
        my_slot = lax.rem(me, sources)

    def source_of(piece, slot):
        if pieces == 1:
            return first_source + slot
        return (
            lax.div(slot, piece_width) * seqs + piece * piece_width + lax.rem(slot, piece_width)
        )

    barrier = pltpu.get_barrier_semaphore()

    def greet(step, carry):
        peer = member_of(my_tier + lax.div(step, crowd), lax.rem(step, crowd))

        @pl.when(peer != me)
        def _():
            pl.semaphore_signal(barrier, inc=1, device_id=place(peer), device_id_type=MESH)

        return carry

    owns = my_tier < owners
    lax.fori_loop(0, jnp.where(owns, (tiers - my_tier) * crowd, 0), greet, 0)

    for index, (source, stage) in enumerate(
        ((k_ref, k_stage), (v_ref, v_stage), (q_ref, q_stage))
    ):
        for head in range(heads):
            pltpu.make_async_copy(
                source.at[0, :, :, pl.ds(head * HEAD, HEAD)],
                stage.at[head],
                stage_sems.at[index],
            ).start()
    small_copies = (
        pltpu.make_async_copy(slot_hbm, slot_ref, stage_sems.at[3]),
        pltpu.make_async_copy(level_hbm, noise_ref, stage_sems.at[4]),
    ) + tuple(
        pltpu.make_async_copy(
            gate_ref.at[:, columns(head, heads_per)], gate_held.at[member], stage_sems.at[5 + member]
        )
        for member, head in enumerate(served)
    )
    for small_copy in small_copies:
        small_copy.start()

    pl.semaphore_wait(barrier, jnp.where(owns, (my_tier + 1) * crowd - 1, owners * crowd))

    def announce(step, carry):
        peer = member_of(lax.div(step, crowd), lax.rem(step, crowd))
        pl.semaphore_signal(
            ready_sems.at[my_tier], inc=1, device_id=place(peer), device_id_type=MESH
        )
        return carry

    lax.fori_loop(0, jnp.where(owns, my_tier * crowd, 0), announce, 0)
    for index, stage in enumerate((k_stage, v_stage, q_stage)):
        pltpu.make_async_copy(stage, stage, stage_sems.at[index]).wait()

    def share(stage, held, send_sem, recv_sem, virtual, peer):
        block = stage.at[pl.ds(virtual * heads_per // copies, heads_per)]

        @pl.when(peer != me)
        def _():
            pltpu.make_async_remote_copy(
                src_ref=block,
                dst_ref=held,
                send_sem=send_sem,
                recv_sem=recv_sem,
                device_id=place(peer),
                device_id_type=MESH,
            ).start()

        @pl.when(peer == me)
        def _():
            pltpu.make_async_copy(block, held, recv_sem).start()

    def each_head(real, send):
        def visit(step, carry):
            index = lax.rem(my_index + step, crowd)
            peer = member_of(real, index)
            send(0, peer, peer)
            if fold:

                @pl.when(real >= owners - fold)
                def _():
                    send(1, member_of(real + fold, index), peer)

            return carry

        lax.fori_loop(0, crowd, visit, 0)

    def send_keys(member, virtual, peer):
        slot = member * devices + me
        share(k_stage, k_held.at[slot], send_sems.at[0], key_sems.at[member], virtual, peer)
        share(v_stage, v_held.at[slot], send_sems.at[1], value_sems.at[member], virtual, peer)

    def send_queries(member, virtual, peer):
        share(
            q_stage,
            q_held.at[member, my_piece, my_slot],
            send_sems.at[2],
            piece_sems.at[member, my_piece],
            virtual,
            peer,
        )

    def send_tier_queries(tier):
        if copies == 1:
            each_head(tier, send_queries)

    known = jnp.minimum(my_tier + 1, owners)

    def below(step, carry):
        each_head(known - 1 - step, send_keys)
        return carry

    def below_queries(step, carry):
        send_tier_queries(known - 1 - step)
        return carry

    def above(tier, carry):
        pl.semaphore_wait(ready_sems.at[tier], crowd)
        each_head(tier, send_keys)
        return carry

    def above_queries(tier, carry):
        send_tier_queries(tier)
        return carry

    lax.fori_loop(0, known, below, 0)
    lax.fori_loop(0, known, below_queries, 0)
    lax.fori_loop(known, owners, above, 0)
    lax.fori_loop(known, owners, above_queries, 0)
    if copies > 1:

        def send_far(index, carry):
            peer = lax.rem(my_slot + index, sources) * copies + my_block
            send_queries(0, peer, peer)
            return carry

        lax.fori_loop(0, sources, send_far, 0)

    for small_copy in small_copies:
        small_copy.wait()
    groups = frames if pieces > 1 else max(1, sources // seqs)
    per_group = per_piece // groups
    position = lax.broadcasted_iota(jnp.int32, (1, key_rows), 1)
    key_frame = lax.div(position, seqs * local_frames * tokens) * local_frames + lax.rem(
        lax.div(position, tokens), local_frames
    )
    key_slot = jnp.zeros((1, key_rows), jnp.int32)
    for group in range(frames):
        for local in range(local_frames):
            key_slot = jnp.where(
                key_frame == group * local_frames + local, slot_ref[group, local], key_slot
            )
    for part in range(groups):
        group = part if pieces > 1 else lax.div(first_source, seqs) + part
        for local in range(local_frames):
            rows = pl.ds(local * tokens, tokens)
            bias[part, rows] = jnp.broadcast_to(
                jnp.where(key_slot <= slot_ref[group, local], 0.0, MASKED), (tokens, key_rows)
            )
            for member in range(members):
                gates[member, part, rows] = jnp.broadcast_to(
                    gate_held[member, pl.ds(noise_ref[group, local], 1), :],
                    (tokens, heads_per * HEAD),
                )

    def arrived(held, semaphore):
        pltpu.make_async_copy(held, held, semaphore).wait()

    def rows_of(block):
        return block.astype(jnp.float32).reshape(-1, HEAD).astype(jnp.bfloat16)

    factor = math.log2(math.e) / math.sqrt(HEAD)
    rows_each = local_frames * tokens

    def attend(member, piece, lane, key_block, value_block):
        scores = lax.dot_general(
            rows_of(q_held[member, piece, :, lane]),
            key_block,
            (((1,), (1,)), ((), ())),
            preferred_element_type=jnp.float32,
        ).reshape(groups, per_group, rows_each, key_rows)
        weights, totals = [], []
        for part in range(groups):
            seen = scores[part] + bias[part][None]
            top = jnp.max(seen, axis=2, keepdims=True)
            weight = jnp.exp2((seen - top) * factor).astype(jnp.bfloat16).astype(jnp.float32)
            totals.append(jnp.sum(weight, axis=2, keepdims=True))
            weights.append(weight)
        weights = jnp.concatenate(weights, axis=0).reshape(-1, key_rows).astype(jnp.bfloat16)
        lanes = slice(lane * HEAD, (lane + 1) * HEAD)
        mixed = jnp.dot(weights, value_block, preferred_element_type=jnp.float32)
        mixed = mixed.reshape(groups, per_group, rows_each, HEAD)
        for part in range(groups):
            result = mixed[part] / totals[part] * gates[member, part, :, lanes][None]
            answer[member, piece, pl.ds(part * per_group, per_group), :, :, lanes] = (
                result.reshape(per_group, local_frames, tokens, HEAD).astype(jnp.bfloat16)
            )

    def give_back(member, piece):
        def send(step, carry):
            slot = lax.rem(my_slot + step, per_piece)
            peer = source_of(piece, slot)
            block = answer.at[member, piece, slot]
            target = out_ref.at[0, :, :, columns(served[member], heads_per)]

            @pl.when(peer != me)
            def _():
                pltpu.make_async_remote_copy(
                    src_ref=block,
                    dst_ref=target,
                    send_sem=send_sems.at[3],
                    recv_sem=out_sem,
                    device_id=place(peer),
                    device_id_type=MESH,
                ).start()

            @pl.when(peer == me)
            def _():
                pltpu.make_async_copy(block, target, out_sem).start()

            return carry

        lax.fori_loop(0, per_piece, send, 0)

    def serve(count):
        key_blocks, value_blocks = [], []
        for member in range(count):
            mine = pl.ds(member * devices, devices)
            arrived(k_held.at[mine], key_sems.at[member])
            arrived(v_held.at[mine], value_sems.at[member])
            key_blocks.append([rows_of(k_held[mine, lane]) for lane in range(heads_per)])
            value_blocks.append([rows_of(v_held[mine, lane]) for lane in range(heads_per)])
        for piece in range(pieces):
            for member in range(count):
                arrived(q_held.at[member, piece], piece_sems.at[member, piece])
                for lane in range(heads_per):
                    attend(
                        member, piece, lane, key_blocks[member][lane], value_blocks[member][lane]
                    )
                give_back(member, piece)

    def sent(index, count):
        view = k_held.at[pl.ds(0, count)]
        pltpu.make_async_copy(view, view, send_sems.at[index]).wait()

    if fold:
        single = my_tier < owners - fold
        double = jnp.logical_and(owns, jnp.logical_not(single))
        pl.when(single)(lambda: serve(1))
        pl.when(double)(lambda: serve(2))
    else:
        serve(1)
    arrived(out_ref, out_sem)

    if fold:

        @pl.when(single)
        def _():
            for index in range(4):
                sent(index, devices - 1)

        @pl.when(double)
        def _():
            for index in range(3):
                sent(index, devices - 2)
            sent(3, 2 * (devices - 1))

        @pl.when(jnp.logical_not(owns))
        def _():
            for index in range(3):
                sent(index, devices)
    else:
        sent(0, devices - 1)
        sent(1, devices - 1)
        if copies == 1:
            sent(2, devices - 1)
            sent(3, devices - 1)
        else:
            home = lax.rem(me, copies) == my_block

            @pl.when(home)
            def _():
                sent(2, sources - 1)
                sent(3, sources - 1)

            @pl.when(jnp.logical_not(home))
            def _():
                sent(2, sources)
                sent(3, sources)


def uneven_kernel(
    plan,
    slot_hbm,
    level_hbm,
    q_ref,
    k_ref,
    v_ref,
    gate_ref,
    out_ref,
    slot_ref,
    noise_ref,
    q_held,
    k_held,
    v_held,
    gate_held,
    bias,
    gates,
    answer,
    small_sems,
    send_sems,
    key_sem,
    value_sem,
    query_sems,
    out_sem,
    ready_sem,
):
    frames, seqs, heads_per = plan
    half, quarter = seqs // 2, seqs // 4
    owning = half + quarter
    devices = frames * seqs
    _, local_frames, tokens, _ = q_ref.shape
    rows_each = local_frames * tokens
    key_rows = devices * rows_each
    my_frame, tier = lax.axis_index("frame"), lax.axis_index("seq")
    me = tier * frames + my_frame
    narrow, wide = heads_per * HEAD, 2 * heads_per * HEAD
    lower = tier < half
    owns_wide = jnp.logical_and(tier >= half, tier < owning)
    last = tier >= owning

    def low_columns(its_tier, frame):
        start = (its_tier * frames + frame) * narrow
        return pl.ds(pl.multiple_of(start, HEAD), narrow)

    def high_columns(its_tier, frame):
        start = half * frames * narrow + ((its_tier - half) * frames + frame) * wide
        return pl.ds(pl.multiple_of(start, HEAD), wide)

    barrier = pltpu.get_barrier_semaphore()

    def signal(semaphore, its_tier, frame):
        place = {"frame": frame, "seq": its_tier}
        pl.semaphore_signal(semaphore, inc=1, device_id=place, device_id_type=MESH)

    @pl.when(jnp.logical_not(last))
    def _():
        def greet(step, carry):
            for frame in range(frames):
                signal(barrier, step + (step >= tier), frame)
            return carry

        lax.fori_loop(0, seqs - 1, greet, 0)
        for other in range(1, frames):
            signal(barrier, tier, lax.rem(my_frame + other, frames))

    small_copies = (
        pltpu.make_async_copy(slot_hbm, slot_ref, small_sems.at[0]),
        pltpu.make_async_copy(level_hbm, noise_ref, small_sems.at[1]),
    )

    def take_own(columns, size):
        for small_copy in small_copies:
            small_copy.start()
        lanes = pl.ds(0, size)
        both = (slice(None), pl.ds(columns.start, wide))
        pltpu.make_async_copy(gate_ref.at[both], gate_held, small_sems.at[2]).start()
        mine = (0, slice(None), slice(None), columns)
        held = (me, slice(None), slice(None), lanes)
        pltpu.make_async_copy(k_ref.at[mine], k_held.at[held], key_sem).start()
        pltpu.make_async_copy(v_ref.at[mine], v_held.at[held], value_sem).start()
        pltpu.make_async_copy(q_ref.at[mine], q_held.at[held], query_sems.at[tier]).start()

    pl.when(lower)(lambda: take_own(low_columns(tier, my_frame), narrow))
    pl.when(owns_wide)(lambda: take_own(high_columns(tier, my_frame), wide))

    pl.semaphore_wait(barrier, owning * frames - jnp.where(last, 0, 1))

    def arrived(held, semaphore):
        pltpu.make_async_copy(held, held, semaphore).wait()

    def push(source, target, send_sem, recv_sem, its_tier, frame):
        pltpu.make_async_remote_copy(
            src_ref=source,
            dst_ref=target,
            send_sem=send_sem,
            recv_sem=recv_sem,
            device_id={"frame": frame, "seq": its_tier},
            device_id_type=MESH,
        ).start()

    def blocks_for(high, its_tier, frame):
        columns = high_columns(its_tier, frame) if high else low_columns(its_tier, frame)
        lanes = pl.ds(0, wide if high else narrow)
        return (0, slice(None), slice(None), columns), (me, slice(None), slice(None), lanes)

    def send_keys(high, its_tier, frame):
        block, held = blocks_for(high, its_tier, frame)
        push(k_ref.at[block], k_held.at[held], send_sems.at[0], key_sem, its_tier, frame)
        push(v_ref.at[block], v_held.at[held], send_sems.at[1], value_sem, its_tier, frame)

    def send_queries(high, its_tier, frame):
        block, held = blocks_for(high, its_tier, frame)
        push(
            q_ref.at[block], q_held.at[held], send_sems.at[2], query_sems.at[tier], its_tier, frame
        )

    def to_low(send):
        for step in range(half):
            for frame in range(frames):
                send(False, jnp.int32(step), frame)

    def to_high(send):
        for step in range(quarter):
            for frame in range(frames):
                send(True, jnp.int32(half + step), frame)

    def beside(send, high, base, count):
        for step in range(count - 1):
            its_tier = base + step + (base + step >= tier)
            for frame in range(frames):
                send(high, its_tier, frame)
        for other in range(1, frames):
            send(high, tier, lax.rem(my_frame + other, frames))

    @pl.when(tier < quarter)
    def _():
        to_high(send_keys)
        to_high(send_queries)
        beside(send_keys, False, 0, half)
        beside(send_queries, False, 0, half)

    @pl.when(jnp.logical_and(tier >= quarter, lower))
    def _():
        to_high(send_keys)
        beside(send_keys, False, 0, half)
        beside(send_queries, False, 0, half)
        to_high(send_queries)

    @pl.when(owns_wide)
    def _():
        to_low(send_keys)
        beside(send_keys, True, half, quarter)
        to_low(send_queries)
        beside(send_queries, True, half, quarter)

    @pl.when(last)
    def _():
        to_low(send_keys)
        to_high(send_keys)
        to_low(send_queries)
        to_high(send_queries)


    @pl.when(last)
    def _():
        def announce(step, carry):
            for frame in range(frames):
                signal(ready_sem, step, frame)
            return carry

        lax.fori_loop(0, owning, announce, 0)

    def rows_of(block):
        return block.astype(jnp.float32).reshape(-1, HEAD).astype(jnp.bfloat16)

    factor = math.log2(math.e) / math.sqrt(HEAD)

    def serve(columns, size, order):
        for small_copy in small_copies:
            small_copy.wait()
        arrived(gate_held, small_sems.at[2])
        position = lax.broadcasted_iota(jnp.int32, (1, key_rows), 1)
        source = lax.div(position, rows_each)
        key_frame = lax.rem(source, frames) * local_frames + lax.rem(
            lax.div(position, tokens), local_frames
        )
        key_slot = jnp.zeros((1, key_rows), jnp.int32)
        for group in range(frames):
            for local in range(local_frames):
                key_slot = jnp.where(
                    key_frame == group * local_frames + local, slot_ref[group, local], key_slot
                )
        for group in range(frames):
            for local in range(local_frames):
                rows = pl.ds(local * tokens, tokens)
                bias[group, rows] = jnp.broadcast_to(
                    jnp.where(key_slot <= slot_ref[group, local], 0.0, MASKED), (tokens, key_rows)
                )
                gates[group, rows] = jnp.broadcast_to(
                    gate_held[pl.ds(noise_ref[group, local], 1), :], (tokens, wide)
                )

        lanes_of = [slice(start, start + HEAD) for start in range(0, size, HEAD)]
        held_lanes = pl.ds(0, size)
        pl.semaphore_wait(ready_sem, quarter * frames)
        arrived(k_held.at[:, :, :, held_lanes], key_sem)
        key_blocks = [rows_of(k_held[:, :, :, lanes]) for lanes in lanes_of]
        arrived(v_held.at[:, :, :, held_lanes], value_sem)
        value_blocks = [rows_of(v_held[:, :, :, lanes]) for lanes in lanes_of]
        target = out_ref.at[0, :, :, columns]

        def attend(first, count):
            for index in range(count):
                blocks = q_held.at[pl.ds((first + index) * frames, frames), :, :, held_lanes]
                arrived(blocks, query_sems.at[first + index])
            pieces = pl.ds(first * frames, count * frames)
            for lanes, key_block, value_block in zip(lanes_of, key_blocks, value_blocks):
                scores = lax.dot_general(
                    rows_of(q_held[pieces, :, :, lanes]),
                    key_block,
                    (((1,), (1,)), ((), ())),
                    preferred_element_type=jnp.float32,
                ).reshape(count, frames, rows_each, key_rows)
                seen = scores + bias[...][None]
                top = jnp.max(seen, axis=3, keepdims=True)
                weights = jnp.exp2((seen - top) * factor).astype(jnp.bfloat16).astype(jnp.float32)
                total = jnp.sum(weights, axis=3, keepdims=True)
                mixed = jnp.dot(
                    weights.reshape(-1, key_rows).astype(jnp.bfloat16),
                    value_block,
                    preferred_element_type=jnp.float32,
                ).reshape(count, frames, rows_each, HEAD)
                result = mixed / total * gates[:, :, lanes][None]
                answer[pieces, :, :, lanes] = result.reshape(
                    count * frames, local_frames, tokens, HEAD
                ).astype(jnp.bfloat16)

        def give_back(its_tier, frame):
            block = answer.at[its_tier * frames + frame, :, :, held_lanes]
            push(block, target, send_sems.at[3], out_sem, its_tier, frame)

        def reply(first, count):
            for step in range(count):
                for frame in range(frames):
                    give_back(jnp.int32(first + step), frame)

        def reply_beside(first, count):
            for step in range(count - 1):
                its_tier = first + step + (first + step >= tier)
                for frame in range(frames):
                    give_back(its_tier, frame)
            for other in range(1, frames):
                give_back(tier, lax.rem(my_frame + other, frames))
            block = answer.at[me, :, :, held_lanes]
            pltpu.make_async_copy(block, target, out_sem).start()

        for first, count, holds_me in order:
            attend(first, count)
            (reply_beside if holds_me else reply)(first, count)

    @pl.when(lower)
    def _():
        order = ((0, half, True), (owning, quarter, False), (half, quarter, False))
        serve(low_columns(tier, my_frame), narrow, order)

    @pl.when(owns_wide)
    def _():
        order = ((0, quarter, False), (quarter, quarter, False), (half, half, True))
        serve(high_columns(tier, my_frame), wide, order)


    arrived(out_ref, out_sem)

    def sent(index, count, size):
        others = answer.at[pl.ds(0, count), :, :, pl.ds(0, size)]
        pltpu.make_async_copy(others, others, send_sems.at[index]).wait()

    def sent_inputs(count):
        for index in range(3):
            sent(index, count, narrow)

    @pl.when(lower)
    def _():
        sent_inputs(devices - 1)
        sent(3, devices - 1, narrow)

    @pl.when(owns_wide)
    def _():
        sent_inputs(devices - 2)
        sent(3, devices - 1, wide)

    pl.when(last)(lambda: sent_inputs(devices))


def uneven_call(plan, queries, keys, values, slot_of, level_of, gate_table):
    frames, seqs, heads_per = plan
    devices = frames * seqs
    _, local_frames, tokens, _ = queries.shape
    features = 2 * heads_per * HEAD
    block = (local_frames, tokens, features)
    rows = local_frames * tokens
    bf16 = jnp.bfloat16
    in_hbm = pl.BlockSpec(memory_space=pltpu.HBM)
    return pl.pallas_call(
        functools.partial(uneven_kernel, plan),
        out_shape=pltpu.VMEM(queries.shape, bf16),
        in_specs=[in_hbm] * 6,
        out_specs=pl.BlockSpec(memory_space=pl.ANY),
        scratch_shapes=[
            pltpu.SMEM(slot_of.shape, jnp.int32),
            pltpu.SMEM(level_of.shape, jnp.int32),
            pltpu.VMEM((devices,) + block, bf16),
            pltpu.VMEM((devices,) + block, bf16),
            pltpu.VMEM((devices,) + block, bf16),
            pltpu.VMEM((gate_table.shape[0], features), jnp.float32),
            pltpu.VMEM((frames, rows, devices * rows), jnp.float32),
            pltpu.VMEM((frames, rows, features), jnp.float32),
            pltpu.VMEM((devices,) + block, bf16),
            pltpu.SemaphoreType.DMA((3,)),
            pltpu.SemaphoreType.DMA((4,)),
            pltpu.SemaphoreType.DMA,
            pltpu.SemaphoreType.DMA,
            pltpu.SemaphoreType.DMA((seqs,)),
            pltpu.SemaphoreType.DMA,
            pltpu.SemaphoreType.REGULAR,
        ],
        compiler_params=pltpu.CompilerParams(collective_id=0, has_side_effects=True),
    )(slot_of, level_of, queries, keys, values, gate_table)


def solution(mesh):
    frames, seqs = mesh.shape["frame"], mesh.shape["seq"]
    devices = frames * seqs

    def body(queries, keys, values, slot_of, level_of, gate_table):
        _, local_frames, tokens, features = queries.shape
        heads = features // HEAD
        heads_per = max(1, heads // devices)
        copies = max(1, devices // heads)
        sources = devices // copies
        if seqs % 4 == 0 and heads % devices == 0:
            uneven_plan = (frames, seqs, heads // devices)
            return uneven_call(
                uneven_plan, queries, keys, values, slot_of, level_of, gate_table
            )
        tiers = math.gcd(8, seqs)
        pieces = math.gcd(8, seqs) if copies == 1 else 1
        fold = 0
        members = 2 if fold else 1
        plan = (frames, seqs, heads, heads_per, copies, sources, tiers, pieces, fold)
        block = (local_frames, tokens, HEAD)
        key_rows = devices * local_frames * tokens
        groups = frames if pieces > 1 else max(1, sources // seqs)
        per_piece = sources // pieces
        bf16 = jnp.bfloat16
        in_hbm = pl.BlockSpec(memory_space=pltpu.HBM)
        return pl.pallas_call(
            functools.partial(kernel, plan),
            out_shape=pltpu.VMEM(queries.shape, bf16),
            in_specs=[in_hbm] * 6,
            out_specs=pl.BlockSpec(memory_space=pl.ANY),
            scratch_shapes=[
                pltpu.SMEM(slot_of.shape, jnp.int32),
                pltpu.SMEM(level_of.shape, jnp.int32),
                pltpu.VMEM((heads,) + block, bf16),
                pltpu.VMEM((heads,) + block, bf16),
                pltpu.VMEM((heads,) + block, bf16),
                pltpu.VMEM((members, pieces, per_piece, heads_per) + block, bf16),
                pltpu.VMEM((members * devices, heads_per) + block, bf16),
                pltpu.VMEM((members * devices, heads_per) + block, bf16),
                pltpu.VMEM((members, gate_table.shape[0], heads_per * HEAD), jnp.float32),
                pltpu.VMEM((groups, local_frames * tokens, key_rows), jnp.float32),
                pltpu.VMEM(
                    (members, groups, local_frames * tokens, heads_per * HEAD), jnp.float32
                ),
                pltpu.VMEM(
                    (members, pieces, per_piece, local_frames, tokens, heads_per * HEAD), bf16
                ),
                pltpu.SemaphoreType.DMA((5 + members,)),
                pltpu.SemaphoreType.DMA((4,)),
                pltpu.SemaphoreType.DMA((members,)),
                pltpu.SemaphoreType.DMA((members,)),
                pltpu.SemaphoreType.DMA((members, pieces)),
                pltpu.SemaphoreType.DMA,
                pltpu.SemaphoreType.REGULAR((tiers,)),
            ],
            compiler_params=pltpu.CompilerParams(
                collective_id=0,
                has_side_effects=True,
            ),
        )(slot_of, level_of, queries, keys, values, gate_table)

    return jax.shard_map(
        body,
        mesh=mesh,
        in_specs=(
            P(("rollout", "frame"), None, "seq", None),
            P(("rollout", "frame"), None, "seq", None),
            P(("rollout", "frame"), None, "seq", None),
            P("rollout", None),
            P("rollout", None),
            P(),
        ),
        out_specs=P(("rollout", "frame"), None, "seq", None),
        check_vma=False,
    )
```

```python
import functools
import math

import jax
import jax.numpy as jnp
from jax import lax
from jax.experimental import pallas as pl
from jax.experimental.pallas import tpu as pltpu
from jax.sharding import PartitionSpec as P

HEAD = 128
MESH = pl.DeviceIdType.MESH
MASKED = -1e30


def kernel(
    plan,
    slot_hbm,
    level_hbm,
    q_ref,
    k_ref,
    v_ref,
    gate_ref,
    out_ref,
    slot_ref,
    noise_ref,
    q_stage,
    k_stage,
    v_stage,
    q_held,
    k_held,
    v_held,
    gate_held,
    bias,
    gates,
    answer,
    stage_sems,
    send_sems,
    key_sems,
    value_sems,
    piece_sems,
    out_sem,
    ready_sems,
):
    frames, seqs, heads, heads_per, copies, sources, tiers, pieces, fold = plan
    devices = frames * seqs
    width = seqs // tiers
    crowd = frames * width
    per_piece = sources // pieces
    _, local_frames, tokens, _ = q_ref.shape
    key_rows = devices * local_frames * tokens
    my_frame, my_seq = lax.axis_index("frame"), lax.axis_index("seq")
    me = my_frame * seqs + my_seq
    my_tier = lax.div(my_seq, width)
    my_index = my_frame * width + lax.rem(my_seq, width)
    owners = tiers - fold
    members = 2 if fold else 1
    served = [
        lax.rem(me + member * fold * width, devices) * heads_per // copies
        for member in range(members)
    ]
    first_source = lax.rem(me, copies) * sources
    my_block = lax.div(me, sources)

    def place(device):
        return {"frame": lax.div(device, seqs), "seq": lax.rem(device, seqs)}

    def columns(head, count):
        return pl.ds(pl.multiple_of(head * HEAD, HEAD), count * HEAD)

    def member_of(tier, index):
        return lax.div(index, width) * seqs + tier * width + lax.rem(index, width)

    piece_width = seqs // pieces
    if pieces > 1:
        my_piece = lax.div(my_seq, piece_width)
        my_slot = my_frame * piece_width + lax.rem(my_seq, piece_width)
    else:
        my_piece = 0
        my_slot = lax.rem(me, sources)

    def source_of(piece, slot):
        if pieces == 1:
            return first_source + slot
        return (
            lax.div(slot, piece_width) * seqs + piece * piece_width + lax.rem(slot, piece_width)
        )

    barrier = pltpu.get_barrier_semaphore()

    def greet(step, carry):
        peer = member_of(my_tier + lax.div(step, crowd), lax.rem(step, crowd))

        @pl.when(peer != me)
        def _():
            pl.semaphore_signal(barrier, inc=1, device_id=place(peer), device_id_type=MESH)

        return carry

    owns = my_tier < owners
    lax.fori_loop(0, jnp.where(owns, (tiers - my_tier) * crowd, 0), greet, 0)

    for index, (source, stage) in enumerate(
        ((k_ref, k_stage), (v_ref, v_stage), (q_ref, q_stage))
    ):
        for head in range(heads):
            pltpu.make_async_copy(
                source.at[0, :, :, pl.ds(head * HEAD, HEAD)],
                stage.at[head],
                stage_sems.at[index],
            ).start()
    small_copies = (
        pltpu.make_async_copy(slot_hbm, slot_ref, stage_sems.at[3]),
        pltpu.make_async_copy(level_hbm, noise_ref, stage_sems.at[4]),
    ) + tuple(
        pltpu.make_async_copy(
            gate_ref.at[:, columns(head, heads_per)], gate_held.at[member], stage_sems.at[5 + member]
        )
        for member, head in enumerate(served)
    )
    for small_copy in small_copies:
        small_copy.start()

    pl.semaphore_wait(barrier, jnp.where(owns, (my_tier + 1) * crowd - 1, owners * crowd))

    def announce(step, carry):
        peer = member_of(lax.div(step, crowd), lax.rem(step, crowd))
        pl.semaphore_signal(
            ready_sems.at[my_tier], inc=1, device_id=place(peer), device_id_type=MESH
        )
        return carry

    lax.fori_loop(0, jnp.where(owns, my_tier * crowd, 0), announce, 0)
    for index, stage in enumerate((k_stage, v_stage, q_stage)):
        pltpu.make_async_copy(stage, stage, stage_sems.at[index]).wait()

    def share(stage, held, send_sem, recv_sem, virtual, peer):
        block = stage.at[pl.ds(virtual * heads_per // copies, heads_per)]

        @pl.when(peer != me)
        def _():
            pltpu.make_async_remote_copy(
                src_ref=block,
                dst_ref=held,
                send_sem=send_sem,
                recv_sem=recv_sem,
                device_id=place(peer),
                device_id_type=MESH,
            ).start()

        @pl.when(peer == me)
        def _():
            pltpu.make_async_copy(block, held, recv_sem).start()

    def each_head(real, send):
        def visit(step, carry):
            index = lax.rem(my_index + step, crowd)
            peer = member_of(real, index)
            send(0, peer, peer)
            if fold:

                @pl.when(real >= owners - fold)
                def _():
                    send(1, member_of(real + fold, index), peer)

            return carry

        lax.fori_loop(0, crowd, visit, 0)

    def send_keys(member, virtual, peer):
        slot = member * devices + me
        share(k_stage, k_held.at[slot], send_sems.at[0], key_sems.at[member], virtual, peer)
        share(v_stage, v_held.at[slot], send_sems.at[1], value_sems.at[member], virtual, peer)

    def send_queries(member, virtual, peer):
        share(
            q_stage,
            q_held.at[member, my_piece, my_slot],
            send_sems.at[2],
            piece_sems.at[member, my_piece],
            virtual,
            peer,
        )

    def send_tier_queries(tier):
        if copies == 1:
            each_head(tier, send_queries)

    known = jnp.minimum(my_tier + 1, owners)

    def below(step, carry):
        each_head(known - 1 - step, send_keys)
        return carry

    def below_queries(step, carry):
        send_tier_queries(known - 1 - step)
        return carry

    def above(tier, carry):
        pl.semaphore_wait(ready_sems.at[tier], crowd)
        each_head(tier, send_keys)
        return carry

    def above_queries(tier, carry):
        send_tier_queries(tier)
        return carry

    lax.fori_loop(0, known, below, 0)
    lax.fori_loop(0, known, below_queries, 0)
    lax.fori_loop(known, owners, above, 0)
    lax.fori_loop(known, owners, above_queries, 0)
    if copies > 1:

        def send_far(index, carry):
            peer = lax.rem(my_slot + index, sources) * copies + my_block
            send_queries(0, peer, peer)
            return carry

        lax.fori_loop(0, sources, send_far, 0)

    for small_copy in small_copies:
        small_copy.wait()
    groups = frames if pieces > 1 else max(1, sources // seqs)
    per_group = per_piece // groups
    position = lax.broadcasted_iota(jnp.int32, (1, key_rows), 1)
    key_frame = lax.div(position, seqs * local_frames * tokens) * local_frames + lax.rem(
        lax.div(position, tokens), local_frames
    )
    key_slot = jnp.zeros((1, key_rows), jnp.int32)
    for group in range(frames):
        for local in range(local_frames):
            key_slot = jnp.where(
                key_frame == group * local_frames + local, slot_ref[group, local], key_slot
            )
    for part in range(groups):
        group = part if pieces > 1 else lax.div(first_source, seqs) + part
        for local in range(local_frames):
            rows = pl.ds(local * tokens, tokens)
            bias[part, rows] = jnp.broadcast_to(
                jnp.where(key_slot <= slot_ref[group, local], 0.0, MASKED), (tokens, key_rows)
            )
            for member in range(members):
                gates[member, part, rows] = jnp.broadcast_to(
                    gate_held[member, pl.ds(noise_ref[group, local], 1), :],
                    (tokens, heads_per * HEAD),
                )

    def arrived(held, semaphore):
        pltpu.make_async_copy(held, held, semaphore).wait()

    def rows_of(block):
        return block.astype(jnp.float32).reshape(-1, HEAD).astype(jnp.bfloat16)

    factor = math.log2(math.e) / math.sqrt(HEAD)
    rows_each = local_frames * tokens

    def attend(member, piece, lane, key_block, value_block):
        scores = lax.dot_general(
            rows_of(q_held[member, piece, :, lane]),
            key_block,
            (((1,), (1,)), ((), ())),
            preferred_element_type=jnp.float32,
        ).reshape(groups, per_group, rows_each, key_rows)
        weights, totals = [], []
        for part in range(groups):
            seen = scores[part] + bias[part][None]
            top = jnp.max(seen, axis=2, keepdims=True)
            weight = jnp.exp2((seen - top) * factor).astype(jnp.bfloat16).astype(jnp.float32)
            totals.append(jnp.sum(weight, axis=2, keepdims=True))
            weights.append(weight)
        weights = jnp.concatenate(weights, axis=0).reshape(-1, key_rows).astype(jnp.bfloat16)
        lanes = slice(lane * HEAD, (lane + 1) * HEAD)
        mixed = jnp.dot(weights, value_block, preferred_element_type=jnp.float32)
        mixed = mixed.reshape(groups, per_group, rows_each, HEAD)
        for part in range(groups):
            result = mixed[part] / totals[part] * gates[member, part, :, lanes][None]
            answer[member, piece, pl.ds(part * per_group, per_group), :, :, lanes] = (
                result.reshape(per_group, local_frames, tokens, HEAD).astype(jnp.bfloat16)
            )

    def give_back(member, piece):
        def send(step, carry):
            slot = lax.rem(my_slot + step, per_piece)
            peer = source_of(piece, slot)
            block = answer.at[member, piece, slot]
            target = out_ref.at[0, :, :, columns(served[member], heads_per)]

            @pl.when(peer != me)
            def _():
                pltpu.make_async_remote_copy(
                    src_ref=block,
                    dst_ref=target,
                    send_sem=send_sems.at[3],
                    recv_sem=out_sem,
                    device_id=place(peer),
                    device_id_type=MESH,
                ).start()

            @pl.when(peer == me)
            def _():
                pltpu.make_async_copy(block, target, out_sem).start()

            return carry

        lax.fori_loop(0, per_piece, send, 0)

    def serve(count):
        key_blocks, value_blocks = [], []
        for member in range(count):
            mine = pl.ds(member * devices, devices)
            arrived(k_held.at[mine], key_sems.at[member])
            arrived(v_held.at[mine], value_sems.at[member])
            key_blocks.append([rows_of(k_held[mine, lane]) for lane in range(heads_per)])
            value_blocks.append([rows_of(v_held[mine, lane]) for lane in range(heads_per)])
        for piece in range(pieces):
            for member in range(count):
                arrived(q_held.at[member, piece], piece_sems.at[member, piece])
                for lane in range(heads_per):
                    attend(
                        member, piece, lane, key_blocks[member][lane], value_blocks[member][lane]
                    )
                give_back(member, piece)

    def sent(index, count):
        view = k_held.at[pl.ds(0, count)]
        pltpu.make_async_copy(view, view, send_sems.at[index]).wait()

    if fold:
        single = my_tier < owners - fold
        double = jnp.logical_and(owns, jnp.logical_not(single))
        pl.when(single)(lambda: serve(1))
        pl.when(double)(lambda: serve(2))
    else:
        serve(1)
    arrived(out_ref, out_sem)

    if fold:

        @pl.when(single)
        def _():
            for index in range(4):
                sent(index, devices - 1)

        @pl.when(double)
        def _():
            for index in range(3):
                sent(index, devices - 2)
            sent(3, 2 * (devices - 1))

        @pl.when(jnp.logical_not(owns))
        def _():
            for index in range(3):
                sent(index, devices)
    else:
        sent(0, devices - 1)
        sent(1, devices - 1)
        if copies == 1:
            sent(2, devices - 1)
            sent(3, devices - 1)
        else:
            home = lax.rem(me, copies) == my_block

            @pl.when(home)
            def _():
                sent(2, sources - 1)
                sent(3, sources - 1)

            @pl.when(jnp.logical_not(home))
            def _():
                sent(2, sources)
                sent(3, sources)


def uneven_kernel(
    plan,
    slot_hbm,
    level_hbm,
    q_ref,
    k_ref,
    v_ref,
    gate_ref,
    out_ref,
    slot_ref,
    noise_ref,
    q_held,
    k_held,
    v_held,
    gate_held,
    bias,
    gates,
    answer,
    small_sems,
    send_sems,
    key_sem,
    value_sem,
    query_sems,
    out_sem,
    ready_sem,
):
    frames, seqs, heads_per = plan
    half, quarter = seqs // 2, seqs // 4
    owning = half + quarter
    devices = frames * seqs
    _, local_frames, tokens, _ = q_ref.shape
    rows_each = local_frames * tokens
    key_rows = devices * rows_each
    my_frame, tier = lax.axis_index("frame"), lax.axis_index("seq")
    me = tier * frames + my_frame
    narrow, wide = heads_per * HEAD, 2 * heads_per * HEAD
    lower = tier < half
    owns_wide = jnp.logical_and(tier >= half, tier < owning)
    last = tier >= owning

    def low_columns(its_tier, frame):
        start = (its_tier * frames + frame) * narrow
        return pl.ds(pl.multiple_of(start, HEAD), narrow)

    def high_columns(its_tier, frame):
        start = half * frames * narrow + ((its_tier - half) * frames + frame) * wide
        return pl.ds(pl.multiple_of(start, HEAD), wide)

    barrier = pltpu.get_barrier_semaphore()

    def signal(semaphore, its_tier, frame):
        place = {"frame": frame, "seq": its_tier}
        pl.semaphore_signal(semaphore, inc=1, device_id=place, device_id_type=MESH)

    @pl.when(jnp.logical_not(last))
    def _():
        def greet(step, carry):
            for frame in range(frames):
                signal(barrier, step + (step >= tier), frame)
            return carry

        lax.fori_loop(0, seqs - 1, greet, 0)
        for other in range(1, frames):
            signal(barrier, tier, lax.rem(my_frame + other, frames))

    small_copies = (
        pltpu.make_async_copy(slot_hbm, slot_ref, small_sems.at[0]),
        pltpu.make_async_copy(level_hbm, noise_ref, small_sems.at[1]),
    )

    def take_own(columns, size):
        for small_copy in small_copies:
            small_copy.start()
        lanes = pl.ds(0, size)
        both = (slice(None), pl.ds(columns.start, wide))
        pltpu.make_async_copy(gate_ref.at[both], gate_held, small_sems.at[2]).start()
        mine = (0, slice(None), slice(None), columns)
        held = (me, slice(None), slice(None), lanes)
        pltpu.make_async_copy(k_ref.at[mine], k_held.at[held], key_sem).start()
        pltpu.make_async_copy(v_ref.at[mine], v_held.at[held], value_sem).start()
        pltpu.make_async_copy(q_ref.at[mine], q_held.at[held], query_sems.at[tier]).start()

    pl.when(lower)(lambda: take_own(low_columns(tier, my_frame), narrow))
    pl.when(owns_wide)(lambda: take_own(high_columns(tier, my_frame), wide))

    pl.semaphore_wait(barrier, owning * frames - jnp.where(last, 0, 1))

    def arrived(held, semaphore):
        pltpu.make_async_copy(held, held, semaphore).wait()

    def push(source, target, send_sem, recv_sem, its_tier, frame):
        pltpu.make_async_remote_copy(
            src_ref=source,
            dst_ref=target,
            send_sem=send_sem,
            recv_sem=recv_sem,
            device_id={"frame": frame, "seq": its_tier},
            device_id_type=MESH,
        ).start()

    def blocks_for(high, its_tier, frame):
        columns = high_columns(its_tier, frame) if high else low_columns(its_tier, frame)
        lanes = pl.ds(0, wide if high else narrow)
        return (0, slice(None), slice(None), columns), (me, slice(None), slice(None), lanes)

    def send_keys(high, its_tier, frame):
        block, held = blocks_for(high, its_tier, frame)
        push(k_ref.at[block], k_held.at[held], send_sems.at[0], key_sem, its_tier, frame)
        push(v_ref.at[block], v_held.at[held], send_sems.at[1], value_sem, its_tier, frame)

    def send_queries(high, its_tier, frame):
        block, held = blocks_for(high, its_tier, frame)
        push(
            q_ref.at[block], q_held.at[held], send_sems.at[2], query_sems.at[tier], its_tier, frame
        )

    def to_low(send):
        for step in range(half):
            for frame in range(frames):
                send(False, jnp.int32(step), frame)

    def to_high(send):
        for step in range(quarter):
            for frame in range(frames):
                send(True, jnp.int32(half + step), frame)

    def beside(send, high, base, count):
        for step in range(count - 1):
            its_tier = base + step + (base + step >= tier)
            for frame in range(frames):
                send(high, its_tier, frame)
        for other in range(1, frames):
            send(high, tier, lax.rem(my_frame + other, frames))

    @pl.when(tier < quarter)
    def _():
        beside(send_keys, False, 0, half)
        to_high(send_keys)
        to_high(send_queries)
        beside(send_queries, False, 0, half)

    @pl.when(jnp.logical_and(tier >= quarter, lower))
    def _():
        to_high(send_keys)
        beside(send_keys, False, 0, half)
        beside(send_queries, False, 0, half)
        to_high(send_queries)

    @pl.when(owns_wide)
    def _():
        to_low(send_keys)
        beside(send_keys, True, half, quarter)
        to_low(send_queries)
        beside(send_queries, True, half, quarter)

    @pl.when(last)
    def _():
        to_high(send_keys)
        to_low(send_keys)
        to_low(send_queries)
        to_high(send_queries)


    @pl.when(last)
    def _():
        def announce(step, carry):
            for frame in range(frames):
                signal(ready_sem, step, frame)
            return carry

        lax.fori_loop(0, owning, announce, 0)

    def rows_of(block):
        return block.astype(jnp.float32).reshape(-1, HEAD).astype(jnp.bfloat16)

    factor = math.log2(math.e) / math.sqrt(HEAD)

    def serve(columns, size, order):
        for small_copy in small_copies:
            small_copy.wait()
        arrived(gate_held, small_sems.at[2])
        position = lax.broadcasted_iota(jnp.int32, (1, key_rows), 1)
        source = lax.div(position, rows_each)
        key_frame = lax.rem(source, frames) * local_frames + lax.rem(
            lax.div(position, tokens), local_frames
        )
        key_slot = jnp.zeros((1, key_rows), jnp.int32)
        for group in range(frames):
            for local in range(local_frames):
                key_slot = jnp.where(
                    key_frame == group * local_frames + local, slot_ref[group, local], key_slot
                )
        for group in range(frames):
            for local in range(local_frames):
                rows = pl.ds(local * tokens, tokens)
                bias[group, rows] = jnp.broadcast_to(
                    jnp.where(key_slot <= slot_ref[group, local], 0.0, MASKED), (tokens, key_rows)
                )
                gates[group, rows] = jnp.broadcast_to(
                    gate_held[pl.ds(noise_ref[group, local], 1), :], (tokens, wide)
                )

        lanes_of = [slice(start, start + HEAD) for start in range(0, size, HEAD)]
        held_lanes = pl.ds(0, size)
        pl.semaphore_wait(ready_sem, quarter * frames)
        arrived(k_held.at[:, :, :, held_lanes], key_sem)
        key_blocks = [rows_of(k_held[:, :, :, lanes]) for lanes in lanes_of]
        arrived(v_held.at[:, :, :, held_lanes], value_sem)
        value_blocks = [rows_of(v_held[:, :, :, lanes]) for lanes in lanes_of]
        target = out_ref.at[0, :, :, columns]

        def attend(first, count):
            for index in range(count):
                blocks = q_held.at[pl.ds((first + index) * frames, frames), :, :, held_lanes]
                arrived(blocks, query_sems.at[first + index])
            pieces = pl.ds(first * frames, count * frames)
            for lanes, key_block, value_block in zip(lanes_of, key_blocks, value_blocks):
                scores = lax.dot_general(
                    rows_of(q_held[pieces, :, :, lanes]),
                    key_block,
                    (((1,), (1,)), ((), ())),
                    preferred_element_type=jnp.float32,
                ).reshape(count, frames, rows_each, key_rows)
                seen = scores + bias[...][None]
                top = jnp.max(seen, axis=3, keepdims=True)
                weights = jnp.exp2((seen - top) * factor).astype(jnp.bfloat16).astype(jnp.float32)
                total = jnp.sum(weights, axis=3, keepdims=True)
                mixed = jnp.dot(
                    weights.reshape(-1, key_rows).astype(jnp.bfloat16),
                    value_block,
                    preferred_element_type=jnp.float32,
                ).reshape(count, frames, rows_each, HEAD)
                result = mixed / total * gates[:, :, lanes][None]
                answer[pieces, :, :, lanes] = result.reshape(
                    count * frames, local_frames, tokens, HEAD
                ).astype(jnp.bfloat16)

        def give_back(its_tier, frame):
            block = answer.at[its_tier * frames + frame, :, :, held_lanes]
            push(block, target, send_sems.at[3], out_sem, its_tier, frame)

        def reply(first, count):
            for step in range(count):
                for frame in range(frames):
                    give_back(jnp.int32(first + step), frame)

        def reply_beside(first, count):
            for step in range(count - 1):
                its_tier = first + step + (first + step >= tier)
                for frame in range(frames):
                    give_back(its_tier, frame)
            for other in range(1, frames):
                give_back(tier, lax.rem(my_frame + other, frames))
            block = answer.at[me, :, :, held_lanes]
            pltpu.make_async_copy(block, target, out_sem).start()

        for first, count, holds_me in order:
            attend(first, count)
            (reply_beside if holds_me else reply)(first, count)

    @pl.when(lower)
    def _():
        order = ((0, half, True), (owning, quarter, False), (half, quarter, False))
        serve(low_columns(tier, my_frame), narrow, order)

    @pl.when(owns_wide)
    def _():
        order = ((0, quarter, False), (quarter, quarter, False), (half, half, True))
        serve(high_columns(tier, my_frame), wide, order)


    arrived(out_ref, out_sem)

    def sent(index, count, size):
        others = answer.at[pl.ds(0, count), :, :, pl.ds(0, size)]
        pltpu.make_async_copy(others, others, send_sems.at[index]).wait()

    def sent_inputs(count):
        for index in range(3):
            sent(index, count, narrow)

    @pl.when(lower)
    def _():
        sent_inputs(devices - 1)
        sent(3, devices - 1, narrow)

    @pl.when(owns_wide)
    def _():
        sent_inputs(devices - 2)
        sent(3, devices - 1, wide)

    pl.when(last)(lambda: sent_inputs(devices))


def uneven_call(plan, queries, keys, values, slot_of, level_of, gate_table):
    frames, seqs, heads_per = plan
    devices = frames * seqs
    _, local_frames, tokens, _ = queries.shape
    features = 2 * heads_per * HEAD
    block = (local_frames, tokens, features)
    rows = local_frames * tokens
    bf16 = jnp.bfloat16
    in_hbm = pl.BlockSpec(memory_space=pltpu.HBM)
    return pl.pallas_call(
        functools.partial(uneven_kernel, plan),
        out_shape=pltpu.VMEM(queries.shape, bf16),
        in_specs=[in_hbm] * 6,
        out_specs=pl.BlockSpec(memory_space=pl.ANY),
        scratch_shapes=[
            pltpu.SMEM(slot_of.shape, jnp.int32),
            pltpu.SMEM(level_of.shape, jnp.int32),
            pltpu.VMEM((devices,) + block, bf16),
            pltpu.VMEM((devices,) + block, bf16),
            pltpu.VMEM((devices,) + block, bf16),
            pltpu.VMEM((gate_table.shape[0], features), jnp.float32),
            pltpu.VMEM((frames, rows, devices * rows), jnp.float32),
            pltpu.VMEM((frames, rows, features), jnp.float32),
            pltpu.VMEM((devices,) + block, bf16),
            pltpu.SemaphoreType.DMA((3,)),
            pltpu.SemaphoreType.DMA((4,)),
            pltpu.SemaphoreType.DMA,
            pltpu.SemaphoreType.DMA,
            pltpu.SemaphoreType.DMA((seqs,)),
            pltpu.SemaphoreType.DMA,
            pltpu.SemaphoreType.REGULAR,
        ],
        compiler_params=pltpu.CompilerParams(collective_id=0, has_side_effects=True),
    )(slot_of, level_of, queries, keys, values, gate_table)


def solution(mesh):
    frames, seqs = mesh.shape["frame"], mesh.shape["seq"]
    devices = frames * seqs

    def body(queries, keys, values, slot_of, level_of, gate_table):
        _, local_frames, tokens, features = queries.shape
        heads = features // HEAD
        heads_per = max(1, heads // devices)
        copies = max(1, devices // heads)
        sources = devices // copies
        if seqs % 4 == 0 and heads % devices == 0:
            uneven_plan = (frames, seqs, heads // devices)
            return uneven_call(
                uneven_plan, queries, keys, values, slot_of, level_of, gate_table
            )
        tiers = math.gcd(8, seqs)
        pieces = math.gcd(8, seqs) if copies == 1 else 1
        fold = 0
        members = 2 if fold else 1
        plan = (frames, seqs, heads, heads_per, copies, sources, tiers, pieces, fold)
        block = (local_frames, tokens, HEAD)
        key_rows = devices * local_frames * tokens
        groups = frames if pieces > 1 else max(1, sources // seqs)
        per_piece = sources // pieces
        bf16 = jnp.bfloat16
        in_hbm = pl.BlockSpec(memory_space=pltpu.HBM)
        return pl.pallas_call(
            functools.partial(kernel, plan),
            out_shape=pltpu.VMEM(queries.shape, bf16),
            in_specs=[in_hbm] * 6,
            out_specs=pl.BlockSpec(memory_space=pl.ANY),
            scratch_shapes=[
                pltpu.SMEM(slot_of.shape, jnp.int32),
                pltpu.SMEM(level_of.shape, jnp.int32),
                pltpu.VMEM((heads,) + block, bf16),
                pltpu.VMEM((heads,) + block, bf16),
                pltpu.VMEM((heads,) + block, bf16),
                pltpu.VMEM((members, pieces, per_piece, heads_per) + block, bf16),
                pltpu.VMEM((members * devices, heads_per) + block, bf16),
                pltpu.VMEM((members * devices, heads_per) + block, bf16),
                pltpu.VMEM((members, gate_table.shape[0], heads_per * HEAD), jnp.float32),
                pltpu.VMEM((groups, local_frames * tokens, key_rows), jnp.float32),
                pltpu.VMEM(
                    (members, groups, local_frames * tokens, heads_per * HEAD), jnp.float32
                ),
                pltpu.VMEM(
                    (members, pieces, per_piece, local_frames, tokens, heads_per * HEAD), bf16
                ),
                pltpu.SemaphoreType.DMA((5 + members,)),
                pltpu.SemaphoreType.DMA((4,)),
                pltpu.SemaphoreType.DMA((members,)),
                pltpu.SemaphoreType.DMA((members,)),
                pltpu.SemaphoreType.DMA((members, pieces)),
                pltpu.SemaphoreType.DMA,
                pltpu.SemaphoreType.REGULAR((tiers,)),
            ],
            compiler_params=pltpu.CompilerParams(
                collective_id=0,
                has_side_effects=True,
            ),
        )(slot_of, level_of, queries, keys, values, gate_table)

    return jax.shard_map(
        body,
        mesh=mesh,
        in_specs=(
            P(("rollout", "frame"), None, "seq", None),
            P(("rollout", "frame"), None, "seq", None),
            P(("rollout", "frame"), None, "seq", None),
            P("rollout", None),
            P("rollout", None),
            P(),
        ),
        out_specs=P(("rollout", "frame"), None, "seq", None),
        check_vma=False,
    )
```

```python
import functools
import math

import jax
import jax.numpy as jnp
from jax import lax
from jax.experimental import pallas as pl
from jax.experimental.pallas import tpu as pltpu
from jax.sharding import PartitionSpec as P

HEAD = 128
MESH = pl.DeviceIdType.MESH
MASKED = -1e30


def kernel(
    plan,
    slot_hbm,
    level_hbm,
    q_ref,
    k_ref,
    v_ref,
    gate_ref,
    out_ref,
    slot_ref,
    noise_ref,
    q_stage,
    k_stage,
    v_stage,
    q_held,
    k_held,
    v_held,
    gate_held,
    bias,
    gates,
    answer,
    stage_sems,
    send_sems,
    key_sems,
    value_sems,
    piece_sems,
    out_sem,
    ready_sems,
):
    frames, seqs, heads, heads_per, copies, sources, tiers, pieces, fold = plan
    devices = frames * seqs
    width = seqs // tiers
    crowd = frames * width
    per_piece = sources // pieces
    _, local_frames, tokens, _ = q_ref.shape
    key_rows = devices * local_frames * tokens
    my_frame, my_seq = lax.axis_index("frame"), lax.axis_index("seq")
    me = my_frame * seqs + my_seq
    my_tier = lax.div(my_seq, width)
    my_index = my_frame * width + lax.rem(my_seq, width)
    owners = tiers - fold
    members = 2 if fold else 1
    served = [
        lax.rem(me + member * fold * width, devices) * heads_per // copies
        for member in range(members)
    ]
    first_source = lax.rem(me, copies) * sources
    my_block = lax.div(me, sources)

    def place(device):
        return {"frame": lax.div(device, seqs), "seq": lax.rem(device, seqs)}

    def columns(head, count):
        return pl.ds(pl.multiple_of(head * HEAD, HEAD), count * HEAD)

    def member_of(tier, index):
        return lax.div(index, width) * seqs + tier * width + lax.rem(index, width)

    piece_width = seqs // pieces
    if pieces > 1:
        my_piece = lax.div(my_seq, piece_width)
        my_slot = my_frame * piece_width + lax.rem(my_seq, piece_width)
    else:
        my_piece = 0
        my_slot = lax.rem(me, sources)

    def source_of(piece, slot):
        if pieces == 1:
            return first_source + slot
        return (
            lax.div(slot, piece_width) * seqs + piece * piece_width + lax.rem(slot, piece_width)
        )

    barrier = pltpu.get_barrier_semaphore()

    def greet(step, carry):
        peer = member_of(my_tier + lax.div(step, crowd), lax.rem(step, crowd))

        @pl.when(peer != me)
        def _():
            pl.semaphore_signal(barrier, inc=1, device_id=place(peer), device_id_type=MESH)

        return carry

    owns = my_tier < owners
    lax.fori_loop(0, jnp.where(owns, (tiers - my_tier) * crowd, 0), greet, 0)

    for index, (source, stage) in enumerate(
        ((k_ref, k_stage), (v_ref, v_stage), (q_ref, q_stage))
    ):
        for head in range(heads):
            pltpu.make_async_copy(
                source.at[0, :, :, pl.ds(head * HEAD, HEAD)],
                stage.at[head],
                stage_sems.at[index],
            ).start()
    small_copies = (
        pltpu.make_async_copy(slot_hbm, slot_ref, stage_sems.at[3]),
        pltpu.make_async_copy(level_hbm, noise_ref, stage_sems.at[4]),
    ) + tuple(
        pltpu.make_async_copy(
            gate_ref.at[:, columns(head, heads_per)], gate_held.at[member], stage_sems.at[5 + member]
        )
        for member, head in enumerate(served)
    )
    for small_copy in small_copies:
        small_copy.start()

    pl.semaphore_wait(barrier, jnp.where(owns, (my_tier + 1) * crowd - 1, owners * crowd))

    def announce(step, carry):
        peer = member_of(lax.div(step, crowd), lax.rem(step, crowd))
        pl.semaphore_signal(
            ready_sems.at[my_tier], inc=1, device_id=place(peer), device_id_type=MESH
        )
        return carry

    lax.fori_loop(0, jnp.where(owns, my_tier * crowd, 0), announce, 0)
    for index, stage in enumerate((k_stage, v_stage, q_stage)):
        pltpu.make_async_copy(stage, stage, stage_sems.at[index]).wait()

    def share(stage, held, send_sem, recv_sem, virtual, peer):
        block = stage.at[pl.ds(virtual * heads_per // copies, heads_per)]

        @pl.when(peer != me)
        def _():
            pltpu.make_async_remote_copy(
                src_ref=block,
                dst_ref=held,
                send_sem=send_sem,
                recv_sem=recv_sem,
                device_id=place(peer),
                device_id_type=MESH,
            ).start()

        @pl.when(peer == me)
        def _():
            pltpu.make_async_copy(block, held, recv_sem).start()

    def each_head(real, send):
        def visit(step, carry):
            index = lax.rem(my_index + step, crowd)
            peer = member_of(real, index)
            send(0, peer, peer)
            if fold:

                @pl.when(real >= owners - fold)
                def _():
                    send(1, member_of(real + fold, index), peer)

            return carry

        lax.fori_loop(0, crowd, visit, 0)

    def send_keys(member, virtual, peer):
        slot = member * devices + me
        share(k_stage, k_held.at[slot], send_sems.at[0], key_sems.at[member], virtual, peer)
        share(v_stage, v_held.at[slot], send_sems.at[1], value_sems.at[member], virtual, peer)

    def send_queries(member, virtual, peer):
        share(
            q_stage,
            q_held.at[member, my_piece, my_slot],
            send_sems.at[2],
            piece_sems.at[member, my_piece],
            virtual,
            peer,
        )

    def send_tier_queries(tier):
        if copies == 1:
            each_head(tier, send_queries)

    known = jnp.minimum(my_tier + 1, owners)

    def below(step, carry):
        each_head(known - 1 - step, send_keys)
        return carry

    def below_queries(step, carry):
        send_tier_queries(known - 1 - step)
        return carry

    def above(tier, carry):
        pl.semaphore_wait(ready_sems.at[tier], crowd)
        each_head(tier, send_keys)
        return carry

    def above_queries(tier, carry):
        send_tier_queries(tier)
        return carry

    lax.fori_loop(0, known, below, 0)
    lax.fori_loop(0, known, below_queries, 0)
    lax.fori_loop(known, owners, above, 0)
    lax.fori_loop(known, owners, above_queries, 0)
    if copies > 1:

        def send_far(index, carry):
            peer = lax.rem(my_slot + index, sources) * copies + my_block
            send_queries(0, peer, peer)
            return carry

        lax.fori_loop(0, sources, send_far, 0)

    for small_copy in small_copies:
        small_copy.wait()
    groups = frames if pieces > 1 else max(1, sources // seqs)
    per_group = per_piece // groups
    position = lax.broadcasted_iota(jnp.int32, (1, key_rows), 1)
    key_frame = lax.div(position, seqs * local_frames * tokens) * local_frames + lax.rem(
        lax.div(position, tokens), local_frames
    )
    key_slot = jnp.zeros((1, key_rows), jnp.int32)
    for group in range(frames):
        for local in range(local_frames):
            key_slot = jnp.where(
                key_frame == group * local_frames + local, slot_ref[group, local], key_slot
            )
    for part in range(groups):
        group = part if pieces > 1 else lax.div(first_source, seqs) + part
        for local in range(local_frames):
            rows = pl.ds(local * tokens, tokens)
            bias[part, rows] = jnp.broadcast_to(
                jnp.where(key_slot <= slot_ref[group, local], 0.0, MASKED), (tokens, key_rows)
            )
            for member in range(members):
                gates[member, part, rows] = jnp.broadcast_to(
                    gate_held[member, pl.ds(noise_ref[group, local], 1), :],
                    (tokens, heads_per * HEAD),
                )

    def arrived(held, semaphore):
        pltpu.make_async_copy(held, held, semaphore).wait()

    def rows_of(block):
        return block.astype(jnp.float32).reshape(-1, HEAD).astype(jnp.bfloat16)

    factor = math.log2(math.e) / math.sqrt(HEAD)
    rows_each = local_frames * tokens

    def attend(member, piece, lane, key_block, value_block):
        scores = lax.dot_general(
            rows_of(q_held[member, piece, :, lane]),
            key_block,
            (((1,), (1,)), ((), ())),
            preferred_element_type=jnp.float32,
        ).reshape(groups, per_group, rows_each, key_rows)
        weights, totals = [], []
        for part in range(groups):
            seen = scores[part] + bias[part][None]
            top = jnp.max(seen, axis=2, keepdims=True)
            weight = jnp.exp2((seen - top) * factor).astype(jnp.bfloat16).astype(jnp.float32)
            totals.append(jnp.sum(weight, axis=2, keepdims=True))
            weights.append(weight)
        weights = jnp.concatenate(weights, axis=0).reshape(-1, key_rows).astype(jnp.bfloat16)
        lanes = slice(lane * HEAD, (lane + 1) * HEAD)
        mixed = jnp.dot(weights, value_block, preferred_element_type=jnp.float32)
        mixed = mixed.reshape(groups, per_group, rows_each, HEAD)
        for part in range(groups):
            result = mixed[part] / totals[part] * gates[member, part, :, lanes][None]
            answer[member, piece, pl.ds(part * per_group, per_group), :, :, lanes] = (
                result.reshape(per_group, local_frames, tokens, HEAD).astype(jnp.bfloat16)
            )

    def give_back(member, piece):
        def send(step, carry):
            slot = lax.rem(my_slot + step, per_piece)
            peer = source_of(piece, slot)
            block = answer.at[member, piece, slot]
            target = out_ref.at[0, :, :, columns(served[member], heads_per)]

            @pl.when(peer != me)
            def _():
                pltpu.make_async_remote_copy(
                    src_ref=block,
                    dst_ref=target,
                    send_sem=send_sems.at[3],
                    recv_sem=out_sem,
                    device_id=place(peer),
                    device_id_type=MESH,
                ).start()

            @pl.when(peer == me)
            def _():
                pltpu.make_async_copy(block, target, out_sem).start()

            return carry

        lax.fori_loop(0, per_piece, send, 0)

    def serve(count):
        key_blocks, value_blocks = [], []
        for member in range(count):
            mine = pl.ds(member * devices, devices)
            arrived(k_held.at[mine], key_sems.at[member])
            arrived(v_held.at[mine], value_sems.at[member])
            key_blocks.append([rows_of(k_held[mine, lane]) for lane in range(heads_per)])
            value_blocks.append([rows_of(v_held[mine, lane]) for lane in range(heads_per)])
        for piece in range(pieces):
            for member in range(count):
                arrived(q_held.at[member, piece], piece_sems.at[member, piece])
                for lane in range(heads_per):
                    attend(
                        member, piece, lane, key_blocks[member][lane], value_blocks[member][lane]
                    )
                give_back(member, piece)

    def sent(index, count):
        view = k_held.at[pl.ds(0, count)]
        pltpu.make_async_copy(view, view, send_sems.at[index]).wait()

    if fold:
        single = my_tier < owners - fold
        double = jnp.logical_and(owns, jnp.logical_not(single))
        pl.when(single)(lambda: serve(1))
        pl.when(double)(lambda: serve(2))
    else:
        serve(1)
    arrived(out_ref, out_sem)

    if fold:

        @pl.when(single)
        def _():
            for index in range(4):
                sent(index, devices - 1)

        @pl.when(double)
        def _():
            for index in range(3):
                sent(index, devices - 2)
            sent(3, 2 * (devices - 1))

        @pl.when(jnp.logical_not(owns))
        def _():
            for index in range(3):
                sent(index, devices)
    else:
        sent(0, devices - 1)
        sent(1, devices - 1)
        if copies == 1:
            sent(2, devices - 1)
            sent(3, devices - 1)
        else:
            home = lax.rem(me, copies) == my_block

            @pl.when(home)
            def _():
                sent(2, sources - 1)
                sent(3, sources - 1)

            @pl.when(jnp.logical_not(home))
            def _():
                sent(2, sources)
                sent(3, sources)


def uneven_kernel(
    plan,
    slot_hbm,
    level_hbm,
    q_ref,
    k_ref,
    v_ref,
    gate_ref,
    out_ref,
    slot_ref,
    noise_ref,
    q_held,
    k_held,
    v_held,
    gate_held,
    bias,
    gates,
    answer,
    small_sems,
    send_sems,
    key_sem,
    value_sem,
    query_sems,
    out_sem,
    ready_sem,
):
    frames, seqs, heads_per = plan
    half, quarter = seqs // 2, seqs // 4
    owning = half + quarter
    devices = frames * seqs
    _, local_frames, tokens, _ = q_ref.shape
    rows_each = local_frames * tokens
    key_rows = devices * rows_each
    my_frame, tier = lax.axis_index("frame"), lax.axis_index("seq")
    me = tier * frames + my_frame
    narrow, wide = heads_per * HEAD, 2 * heads_per * HEAD
    lower = tier < half
    owns_wide = jnp.logical_and(tier >= half, tier < owning)
    last = tier >= owning

    def low_columns(its_tier, frame):
        start = (its_tier * frames + frame) * narrow
        return pl.ds(pl.multiple_of(start, HEAD), narrow)

    def high_columns(its_tier, frame):
        start = half * frames * narrow + ((its_tier - half) * frames + frame) * wide
        return pl.ds(pl.multiple_of(start, HEAD), wide)

    barrier = pltpu.get_barrier_semaphore()

    def signal(semaphore, its_tier, frame):
        place = {"frame": frame, "seq": its_tier}
        pl.semaphore_signal(semaphore, inc=1, device_id=place, device_id_type=MESH)

    @pl.when(jnp.logical_not(last))
    def _():
        def greet(step, carry):
            for frame in range(frames):
                signal(barrier, step + (step >= tier), frame)
            return carry

        lax.fori_loop(0, seqs - 1, greet, 0)
        for other in range(1, frames):
            signal(barrier, tier, lax.rem(my_frame + other, frames))

    small_copies = (
        pltpu.make_async_copy(slot_hbm, slot_ref, small_sems.at[0]),
        pltpu.make_async_copy(level_hbm, noise_ref, small_sems.at[1]),
    )

    def take_own(columns, size):
        for small_copy in small_copies:
            small_copy.start()
        lanes = pl.ds(0, size)
        both = (slice(None), pl.ds(columns.start, wide))
        pltpu.make_async_copy(gate_ref.at[both], gate_held, small_sems.at[2]).start()
        mine = (0, slice(None), slice(None), columns)
        held = (me, slice(None), slice(None), lanes)
        pltpu.make_async_copy(k_ref.at[mine], k_held.at[held], key_sem).start()
        pltpu.make_async_copy(v_ref.at[mine], v_held.at[held], value_sem).start()
        pltpu.make_async_copy(q_ref.at[mine], q_held.at[held], query_sems.at[tier]).start()

    pl.when(lower)(lambda: take_own(low_columns(tier, my_frame), narrow))
    pl.when(owns_wide)(lambda: take_own(high_columns(tier, my_frame), wide))

    pl.semaphore_wait(barrier, owning * frames - jnp.where(last, 0, 1))

    def arrived(held, semaphore):
        pltpu.make_async_copy(held, held, semaphore).wait()

    def push(source, target, send_sem, recv_sem, its_tier, frame):
        pltpu.make_async_remote_copy(
            src_ref=source,
            dst_ref=target,
            send_sem=send_sem,
            recv_sem=recv_sem,
            device_id={"frame": frame, "seq": its_tier},
            device_id_type=MESH,
        ).start()

    def blocks_for(high, its_tier, frame):
        columns = high_columns(its_tier, frame) if high else low_columns(its_tier, frame)
        lanes = pl.ds(0, wide if high else narrow)
        return (0, slice(None), slice(None), columns), (me, slice(None), slice(None), lanes)

    def send_keys(high, its_tier, frame):
        block, held = blocks_for(high, its_tier, frame)
        push(k_ref.at[block], k_held.at[held], send_sems.at[0], key_sem, its_tier, frame)
        push(v_ref.at[block], v_held.at[held], send_sems.at[1], value_sem, its_tier, frame)

    def send_queries(high, its_tier, frame):
        block, held = blocks_for(high, its_tier, frame)
        push(
            q_ref.at[block], q_held.at[held], send_sems.at[2], query_sems.at[tier], its_tier, frame
        )

    def to_low(send):
        for step in range(half):
            for frame in range(frames):
                send(False, jnp.int32(step), lax.rem(frame + my_frame, frames))

    def to_high(send):
        for step in range(quarter):
            for frame in range(frames):
                send(True, half + (step + lax.rem(tier, 2) * (1 - 2 * (step % 2))), lax.rem(frame + my_frame, frames))

    def beside(send, high, base, count):
        for step in range(count - 1):
            its_tier = base + step + (base + step >= tier)
            for frame in range(frames):
                send(high, its_tier, frame)
        for other in range(1, frames):
            send(high, tier, lax.rem(my_frame + other, frames))

    @pl.when(tier < quarter)
    def _():
        beside(send_keys, False, 0, half)
        to_high(send_keys)
        to_high(send_queries)
        beside(send_queries, False, 0, half)

    @pl.when(jnp.logical_and(tier >= quarter, lower))
    def _():
        to_high(send_keys)
        beside(send_keys, False, 0, half)
        beside(send_queries, False, 0, half)
        to_high(send_queries)

    @pl.when(owns_wide)
    def _():
        to_low(send_keys)
        beside(send_keys, True, half, quarter)
        to_low(send_queries)
        beside(send_queries, True, half, quarter)

    @pl.when(last)
    def _():
        to_high(send_keys)
        to_low(send_keys)
        to_low(send_queries)
        to_high(send_queries)


    @pl.when(last)
    def _():
        def announce(step, carry):
            for frame in range(frames):
                signal(ready_sem, step, frame)
            return carry

        lax.fori_loop(0, owning, announce, 0)

    def rows_of(block):
        return block.astype(jnp.float32).reshape(-1, HEAD).astype(jnp.bfloat16)

    factor = math.log2(math.e) / math.sqrt(HEAD)

    def serve(columns, size, order):
        for small_copy in small_copies:
            small_copy.wait()
        arrived(gate_held, small_sems.at[2])
        position = lax.broadcasted_iota(jnp.int32, (1, key_rows), 1)
        source = lax.div(position, rows_each)
        key_frame = lax.rem(source, frames) * local_frames + lax.rem(
            lax.div(position, tokens), local_frames
        )
        key_slot = jnp.zeros((1, key_rows), jnp.int32)
        for group in range(frames):
            for local in range(local_frames):
                key_slot = jnp.where(
                    key_frame == group * local_frames + local, slot_ref[group, local], key_slot
                )
        for group in range(frames):
            for local in range(local_frames):
                rows = pl.ds(local * tokens, tokens)
                bias[group, rows] = jnp.broadcast_to(
                    jnp.where(key_slot <= slot_ref[group, local], 0.0, MASKED), (tokens, key_rows)
                )
                gates[group, rows] = jnp.broadcast_to(
                    gate_held[pl.ds(noise_ref[group, local], 1), :], (tokens, wide)
                )

        lanes_of = [slice(start, start + HEAD) for start in range(0, size, HEAD)]
        held_lanes = pl.ds(0, size)
        pl.semaphore_wait(ready_sem, quarter * frames)
        arrived(k_held.at[:, :, :, held_lanes], key_sem)
        key_blocks = [rows_of(k_held[:, :, :, lanes]) for lanes in lanes_of]
        arrived(v_held.at[:, :, :, held_lanes], value_sem)
        value_blocks = [rows_of(v_held[:, :, :, lanes]) for lanes in lanes_of]
        target = out_ref.at[0, :, :, columns]

        def attend(first, count):
            for index in range(count):
                blocks = q_held.at[pl.ds((first + index) * frames, frames), :, :, held_lanes]
                arrived(blocks, query_sems.at[first + index])
            pieces = pl.ds(first * frames, count * frames)
            for lanes, key_block, value_block in zip(lanes_of, key_blocks, value_blocks):
                scores = lax.dot_general(
                    rows_of(q_held[pieces, :, :, lanes]),
                    key_block,
                    (((1,), (1,)), ((), ())),
                    preferred_element_type=jnp.float32,
                ).reshape(count, frames, rows_each, key_rows)
                seen = scores + bias[...][None]
                top = jnp.max(seen, axis=3, keepdims=True)
                weights = jnp.exp2((seen - top) * factor).astype(jnp.bfloat16).astype(jnp.float32)
                total = jnp.sum(weights, axis=3, keepdims=True)
                mixed = jnp.dot(
                    weights.reshape(-1, key_rows).astype(jnp.bfloat16),
                    value_block,
                    preferred_element_type=jnp.float32,
                ).reshape(count, frames, rows_each, HEAD)
                result = mixed / total * gates[:, :, lanes][None]
                answer[pieces, :, :, lanes] = result.reshape(
                    count * frames, local_frames, tokens, HEAD
                ).astype(jnp.bfloat16)

        def give_back(its_tier, frame):
            block = answer.at[its_tier * frames + frame, :, :, held_lanes]
            push(block, target, send_sems.at[3], out_sem, its_tier, frame)

        def reply(first, count):
            for step in range(count):
                for frame in range(frames):
                    give_back(jnp.int32(first + step), frame)

        def reply_beside(first, count):
            for step in range(count - 1):
                its_tier = first + step + (first + step >= tier)
                for frame in range(frames):
                    give_back(its_tier, frame)
            for other in range(1, frames):
                give_back(tier, lax.rem(my_frame + other, frames))
            block = answer.at[me, :, :, held_lanes]
            pltpu.make_async_copy(block, target, out_sem).start()

        for first, count, holds_me in order:
            attend(first, count)
            (reply_beside if holds_me else reply)(first, count)

    @pl.when(lower)
    def _():
        order = ((0, half, True), (owning, quarter, False), (half, quarter, False))
        serve(low_columns(tier, my_frame), narrow, order)

    @pl.when(owns_wide)
    def _():
        order = ((0, 1, False), (1, 1, False), (quarter, quarter, False), (half, half, True))
        serve(high_columns(tier, my_frame), wide, order)


    arrived(out_ref, out_sem)

    def sent(index, count, size):
        others = answer.at[pl.ds(0, count), :, :, pl.ds(0, size)]
        pltpu.make_async_copy(others, others, send_sems.at[index]).wait()

    def sent_inputs(count):
        for index in range(3):
            sent(index, count, narrow)

    @pl.when(lower)
    def _():
        sent_inputs(devices - 1)
        sent(3, devices - 1, narrow)

    @pl.when(owns_wide)
    def _():
        sent_inputs(devices - 2)
        sent(3, devices - 1, wide)

    pl.when(last)(lambda: sent_inputs(devices))


def uneven_call(plan, queries, keys, values, slot_of, level_of, gate_table):
    frames, seqs, heads_per = plan
    devices = frames * seqs
    _, local_frames, tokens, _ = queries.shape
    features = 2 * heads_per * HEAD
    block = (local_frames, tokens, features)
    rows = local_frames * tokens
    bf16 = jnp.bfloat16
    in_hbm = pl.BlockSpec(memory_space=pltpu.HBM)
    return pl.pallas_call(
        functools.partial(uneven_kernel, plan),
        out_shape=pltpu.VMEM(queries.shape, bf16),
        in_specs=[in_hbm] * 6,
        out_specs=pl.BlockSpec(memory_space=pl.ANY),
        scratch_shapes=[
            pltpu.SMEM(slot_of.shape, jnp.int32),
            pltpu.SMEM(level_of.shape, jnp.int32),
            pltpu.VMEM((devices,) + block, bf16),
            pltpu.VMEM((devices,) + block, bf16),
            pltpu.VMEM((devices,) + block, bf16),
            pltpu.VMEM((gate_table.shape[0], features), jnp.float32),
            pltpu.VMEM((frames, rows, devices * rows), jnp.float32),
            pltpu.VMEM((frames, rows, features), jnp.float32),
            pltpu.VMEM((devices,) + block, bf16),
            pltpu.SemaphoreType.DMA((3,)),
            pltpu.SemaphoreType.DMA((4,)),
            pltpu.SemaphoreType.DMA,
            pltpu.SemaphoreType.DMA,
            pltpu.SemaphoreType.DMA((seqs,)),
            pltpu.SemaphoreType.DMA,
            pltpu.SemaphoreType.REGULAR,
        ],
        compiler_params=pltpu.CompilerParams(collective_id=0, has_side_effects=True),
    )(slot_of, level_of, queries, keys, values, gate_table)


def solution(mesh):
    frames, seqs = mesh.shape["frame"], mesh.shape["seq"]
    devices = frames * seqs

    def body(queries, keys, values, slot_of, level_of, gate_table):
        _, local_frames, tokens, features = queries.shape
        heads = features // HEAD
        heads_per = max(1, heads // devices)
        copies = max(1, devices // heads)
        sources = devices // copies
        if seqs % 4 == 0 and heads % devices == 0:
            uneven_plan = (frames, seqs, heads // devices)
            return uneven_call(
                uneven_plan, queries, keys, values, slot_of, level_of, gate_table
            )
        tiers = math.gcd(8, seqs)
        pieces = math.gcd(8, seqs) if copies == 1 else 1
        fold = 0
        members = 2 if fold else 1
        plan = (frames, seqs, heads, heads_per, copies, sources, tiers, pieces, fold)
        block = (local_frames, tokens, HEAD)
        key_rows = devices * local_frames * tokens
        groups = frames if pieces > 1 else max(1, sources // seqs)
        per_piece = sources // pieces
        bf16 = jnp.bfloat16
        in_hbm = pl.BlockSpec(memory_space=pltpu.HBM)
        return pl.pallas_call(
            functools.partial(kernel, plan),
            out_shape=pltpu.VMEM(queries.shape, bf16),
            in_specs=[in_hbm] * 6,
            out_specs=pl.BlockSpec(memory_space=pl.ANY),
            scratch_shapes=[
                pltpu.SMEM(slot_of.shape, jnp.int32),
                pltpu.SMEM(level_of.shape, jnp.int32),
                pltpu.VMEM((heads,) + block, bf16),
                pltpu.VMEM((heads,) + block, bf16),
                pltpu.VMEM((heads,) + block, bf16),
                pltpu.VMEM((members, pieces, per_piece, heads_per) + block, bf16),
                pltpu.VMEM((members * devices, heads_per) + block, bf16),
                pltpu.VMEM((members * devices, heads_per) + block, bf16),
                pltpu.VMEM((members, gate_table.shape[0], heads_per * HEAD), jnp.float32),
                pltpu.VMEM((groups, local_frames * tokens, key_rows), jnp.float32),
                pltpu.VMEM(
                    (members, groups, local_frames * tokens, heads_per * HEAD), jnp.float32
                ),
                pltpu.VMEM(
                    (members, pieces, per_piece, local_frames, tokens, heads_per * HEAD), bf16
                ),
                pltpu.SemaphoreType.DMA((5 + members,)),
                pltpu.SemaphoreType.DMA((4,)),
                pltpu.SemaphoreType.DMA((members,)),
                pltpu.SemaphoreType.DMA((members,)),
                pltpu.SemaphoreType.DMA((members, pieces)),
                pltpu.SemaphoreType.DMA,
                pltpu.SemaphoreType.REGULAR((tiers,)),
            ],
            compiler_params=pltpu.CompilerParams(
                collective_id=0,
                has_side_effects=True,
            ),
        )(slot_of, level_of, queries, keys, values, gate_table)

    return jax.shard_map(
        body,
        mesh=mesh,
        in_specs=(
            P(("rollout", "frame"), None, "seq", None),
            P(("rollout", "frame"), None, "seq", None),
            P(("rollout", "frame"), None, "seq", None),
            P("rollout", None),
            P("rollout", None),
            P(),
        ),
        out_specs=P(("rollout", "frame"), None, "seq", None),
        check_vma=False,
    )
```

```python
import functools
import math

import jax
import jax.numpy as jnp
from jax import lax
from jax.experimental import pallas as pl
from jax.experimental.pallas import tpu as pltpu
from jax.sharding import PartitionSpec as P

HEAD = 128
MESH = pl.DeviceIdType.MESH
MASKED = -1e30


def kernel(
    plan,
    slot_hbm,
    level_hbm,
    q_ref,
    k_ref,
    v_ref,
    gate_ref,
    out_ref,
    slot_ref,
    noise_ref,
    q_stage,
    k_stage,
    v_stage,
    q_held,
    k_held,
    v_held,
    gate_held,
    bias,
    gates,
    answer,
    stage_sems,
    send_sems,
    key_sems,
    value_sems,
    piece_sems,
    out_sem,
    ready_sems,
):
    frames, seqs, heads, heads_per, copies, sources, tiers, pieces, fold = plan
    devices = frames * seqs
    width = seqs // tiers
    crowd = frames * width
    per_piece = sources // pieces
    _, local_frames, tokens, _ = q_ref.shape
    key_rows = devices * local_frames * tokens
    my_frame, my_seq = lax.axis_index("frame"), lax.axis_index("seq")
    me = my_frame * seqs + my_seq
    my_tier = lax.div(my_seq, width)
    my_index = my_frame * width + lax.rem(my_seq, width)
    owners = tiers - fold
    members = 2 if fold else 1
    served = [
        lax.rem(me + member * fold * width, devices) * heads_per // copies
        for member in range(members)
    ]
    first_source = lax.rem(me, copies) * sources
    my_block = lax.div(me, sources)

    def place(device):
        return {"frame": lax.div(device, seqs), "seq": lax.rem(device, seqs)}

    def columns(head, count):
        return pl.ds(pl.multiple_of(head * HEAD, HEAD), count * HEAD)

    def member_of(tier, index):
        return lax.div(index, width) * seqs + tier * width + lax.rem(index, width)

    piece_width = seqs // pieces
    if pieces > 1:
        my_piece = lax.div(my_seq, piece_width)
        my_slot = my_frame * piece_width + lax.rem(my_seq, piece_width)
    else:
        my_piece = 0
        my_slot = lax.rem(me, sources)

    def source_of(piece, slot):
        if pieces == 1:
            return first_source + slot
        return (
            lax.div(slot, piece_width) * seqs + piece * piece_width + lax.rem(slot, piece_width)
        )

    barrier = pltpu.get_barrier_semaphore()

    def greet(step, carry):
        peer = member_of(my_tier + lax.div(step, crowd), lax.rem(step, crowd))

        @pl.when(peer != me)
        def _():
            pl.semaphore_signal(barrier, inc=1, device_id=place(peer), device_id_type=MESH)

        return carry

    owns = my_tier < owners
    lax.fori_loop(0, jnp.where(owns, (tiers - my_tier) * crowd, 0), greet, 0)

    for index, (source, stage) in enumerate(
        ((k_ref, k_stage), (v_ref, v_stage), (q_ref, q_stage))
    ):
        for head in range(heads):
            pltpu.make_async_copy(
                source.at[0, :, :, pl.ds(head * HEAD, HEAD)],
                stage.at[head],
                stage_sems.at[index],
            ).start()
    small_copies = (
        pltpu.make_async_copy(slot_hbm, slot_ref, stage_sems.at[3]),
        pltpu.make_async_copy(level_hbm, noise_ref, stage_sems.at[4]),
    ) + tuple(
        pltpu.make_async_copy(
            gate_ref.at[:, columns(head, heads_per)], gate_held.at[member], stage_sems.at[5 + member]
        )
        for member, head in enumerate(served)
    )
    for small_copy in small_copies:
        small_copy.start()

    pl.semaphore_wait(barrier, jnp.where(owns, (my_tier + 1) * crowd - 1, owners * crowd))

    def announce(step, carry):
        peer = member_of(lax.div(step, crowd), lax.rem(step, crowd))
        pl.semaphore_signal(
            ready_sems.at[my_tier], inc=1, device_id=place(peer), device_id_type=MESH
        )
        return carry

    lax.fori_loop(0, jnp.where(owns, my_tier * crowd, 0), announce, 0)
    for index, stage in enumerate((k_stage, v_stage, q_stage)):
        pltpu.make_async_copy(stage, stage, stage_sems.at[index]).wait()

    def share(stage, held, send_sem, recv_sem, virtual, peer):
        block = stage.at[pl.ds(virtual * heads_per // copies, heads_per)]

        @pl.when(peer != me)
        def _():
            pltpu.make_async_remote_copy(
                src_ref=block,
                dst_ref=held,
                send_sem=send_sem,
                recv_sem=recv_sem,
                device_id=place(peer),
                device_id_type=MESH,
            ).start()

        @pl.when(peer == me)
        def _():
            pltpu.make_async_copy(block, held, recv_sem).start()

    def each_head(real, send):
        def visit(step, carry):
            index = lax.rem(my_index + step, crowd)
            peer = member_of(real, index)
            send(0, peer, peer)
            if fold:

                @pl.when(real >= owners - fold)
                def _():
                    send(1, member_of(real + fold, index), peer)

            return carry

        lax.fori_loop(0, crowd, visit, 0)

    def send_keys(member, virtual, peer):
        slot = member * devices + me
        share(k_stage, k_held.at[slot], send_sems.at[0], key_sems.at[member], virtual, peer)
        share(v_stage, v_held.at[slot], send_sems.at[1], value_sems.at[member], virtual, peer)

    def send_queries(member, virtual, peer):
        share(
            q_stage,
            q_held.at[member, my_piece, my_slot],
            send_sems.at[2],
            piece_sems.at[member, my_piece],
            virtual,
            peer,
        )

    def send_tier_queries(tier):
        if copies == 1:
            each_head(tier, send_queries)

    known = jnp.minimum(my_tier + 1, owners)

    def below(step, carry):
        each_head(known - 1 - step, send_keys)
        return carry

    def below_queries(step, carry):
        send_tier_queries(known - 1 - step)
        return carry

    def above(tier, carry):
        pl.semaphore_wait(ready_sems.at[tier], crowd)
        each_head(tier, send_keys)
        return carry

    def above_queries(tier, carry):
        send_tier_queries(tier)
        return carry

    lax.fori_loop(0, known, below, 0)
    lax.fori_loop(0, known, below_queries, 0)
    lax.fori_loop(known, owners, above, 0)
    lax.fori_loop(known, owners, above_queries, 0)
    if copies > 1:

        def send_far(index, carry):
            peer = lax.rem(my_slot + index, sources) * copies + my_block
            send_queries(0, peer, peer)
            return carry

        lax.fori_loop(0, sources, send_far, 0)

    for small_copy in small_copies:
        small_copy.wait()
    groups = frames if pieces > 1 else max(1, sources // seqs)
    per_group = per_piece // groups
    position = lax.broadcasted_iota(jnp.int32, (1, key_rows), 1)
    key_frame = lax.div(position, seqs * local_frames * tokens) * local_frames + lax.rem(
        lax.div(position, tokens), local_frames
    )
    key_slot = jnp.zeros((1, key_rows), jnp.int32)
    for group in range(frames):
        for local in range(local_frames):
            key_slot = jnp.where(
                key_frame == group * local_frames + local, slot_ref[group, local], key_slot
            )
    for part in range(groups):
        group = part if pieces > 1 else lax.div(first_source, seqs) + part
        for local in range(local_frames):
            rows = pl.ds(local * tokens, tokens)
            bias[part, rows] = jnp.broadcast_to(
                jnp.where(key_slot <= slot_ref[group, local], 0.0, MASKED), (tokens, key_rows)
            )
            for member in range(members):
                gates[member, part, rows] = jnp.broadcast_to(
                    gate_held[member, pl.ds(noise_ref[group, local], 1), :],
                    (tokens, heads_per * HEAD),
                )

    def arrived(held, semaphore):
        pltpu.make_async_copy(held, held, semaphore).wait()

    def rows_of(block):
        return block.astype(jnp.float32).reshape(-1, HEAD).astype(jnp.bfloat16)

    factor = math.log2(math.e) / math.sqrt(HEAD)
    rows_each = local_frames * tokens

    def attend(member, piece, lane, key_block, value_block):
        scores = lax.dot_general(
            rows_of(q_held[member, piece, :, lane]),
            key_block,
            (((1,), (1,)), ((), ())),
            preferred_element_type=jnp.float32,
        ).reshape(groups, per_group, rows_each, key_rows)
        weights, totals = [], []
        for part in range(groups):
            seen = scores[part] + bias[part][None]
            top = jnp.max(seen, axis=2, keepdims=True)
            weight = jnp.exp2((seen - top) * factor).astype(jnp.bfloat16).astype(jnp.float32)
            totals.append(jnp.sum(weight, axis=2, keepdims=True))
            weights.append(weight)
        weights = jnp.concatenate(weights, axis=0).reshape(-1, key_rows).astype(jnp.bfloat16)
        lanes = slice(lane * HEAD, (lane + 1) * HEAD)
        mixed = jnp.dot(weights, value_block, preferred_element_type=jnp.float32)
        mixed = mixed.reshape(groups, per_group, rows_each, HEAD)
        for part in range(groups):
            result = mixed[part] / totals[part] * gates[member, part, :, lanes][None]
            answer[member, piece, pl.ds(part * per_group, per_group), :, :, lanes] = (
                result.reshape(per_group, local_frames, tokens, HEAD).astype(jnp.bfloat16)
            )

    def give_back(member, piece):
        def send(step, carry):
            slot = lax.rem(my_slot + step, per_piece)
            peer = source_of(piece, slot)
            block = answer.at[member, piece, slot]
            target = out_ref.at[0, :, :, columns(served[member], heads_per)]

            @pl.when(peer != me)
            def _():
                pltpu.make_async_remote_copy(
                    src_ref=block,
                    dst_ref=target,
                    send_sem=send_sems.at[3],
                    recv_sem=out_sem,
                    device_id=place(peer),
                    device_id_type=MESH,
                ).start()

            @pl.when(peer == me)
            def _():
                pltpu.make_async_copy(block, target, out_sem).start()

            return carry

        lax.fori_loop(0, per_piece, send, 0)

    def serve(count):
        key_blocks, value_blocks = [], []
        for member in range(count):
            mine = pl.ds(member * devices, devices)
            arrived(k_held.at[mine], key_sems.at[member])
            arrived(v_held.at[mine], value_sems.at[member])
            key_blocks.append([rows_of(k_held[mine, lane]) for lane in range(heads_per)])
            value_blocks.append([rows_of(v_held[mine, lane]) for lane in range(heads_per)])
        for piece in range(pieces):
            for member in range(count):
                arrived(q_held.at[member, piece], piece_sems.at[member, piece])
                for lane in range(heads_per):
                    attend(
                        member, piece, lane, key_blocks[member][lane], value_blocks[member][lane]
                    )
                give_back(member, piece)

    def sent(index, count):
        view = k_held.at[pl.ds(0, count)]
        pltpu.make_async_copy(view, view, send_sems.at[index]).wait()

    if fold:
        single = my_tier < owners - fold
        double = jnp.logical_and(owns, jnp.logical_not(single))
        pl.when(single)(lambda: serve(1))
        pl.when(double)(lambda: serve(2))
    else:
        serve(1)
    arrived(out_ref, out_sem)

    if fold:

        @pl.when(single)
        def _():
            for index in range(4):
                sent(index, devices - 1)

        @pl.when(double)
        def _():
            for index in range(3):
                sent(index, devices - 2)
            sent(3, 2 * (devices - 1))

        @pl.when(jnp.logical_not(owns))
        def _():
            for index in range(3):
                sent(index, devices)
    else:
        sent(0, devices - 1)
        sent(1, devices - 1)
        if copies == 1:
            sent(2, devices - 1)
            sent(3, devices - 1)
        else:
            home = lax.rem(me, copies) == my_block

            @pl.when(home)
            def _():
                sent(2, sources - 1)
                sent(3, sources - 1)

            @pl.when(jnp.logical_not(home))
            def _():
                sent(2, sources)
                sent(3, sources)


def uneven_kernel(
    plan,
    slot_hbm,
    level_hbm,
    q_ref,
    k_ref,
    v_ref,
    gate_ref,
    out_ref,
    slot_ref,
    noise_ref,
    q_stage,
    k_stage,
    v_stage,
    q_held,
    k_held,
    v_held,
    gate_held,
    bias,
    gates,
    answer,
    small_sems,
    send_sems,
    key_sem,
    value_sem,
    query_sems,
    out_sem,
    ready_sem,
):
    frames, seqs, heads_per = plan
    half, quarter = seqs // 2, seqs // 4
    owning = half + quarter
    devices = frames * seqs
    _, local_frames, tokens, _ = q_ref.shape
    rows_each = local_frames * tokens
    key_rows = devices * rows_each
    my_frame, tier = lax.axis_index("frame"), lax.axis_index("seq")
    me = tier * frames + my_frame
    narrow, wide = heads_per * HEAD, 2 * heads_per * HEAD
    lower = tier < half
    owns_wide = jnp.logical_and(tier >= half, tier < owning)
    last = tier >= owning

    def low_columns(its_tier, frame):
        start = (its_tier * frames + frame) * narrow
        return pl.ds(pl.multiple_of(start, HEAD), narrow)

    def high_columns(its_tier, frame):
        start = half * frames * narrow + ((its_tier - half) * frames + frame) * wide
        return pl.ds(pl.multiple_of(start, HEAD), wide)

    stage_copies = [
        pltpu.make_async_copy(source, stage, small_sems.at[3 + index])
        for index, (source, stage) in enumerate(
            ((k_ref, k_stage), (v_ref, v_stage), (q_ref, q_stage))
        )
    ]
    for stage_copy in stage_copies:
        stage_copy.start()

    barrier = pltpu.get_barrier_semaphore()

    def signal(semaphore, its_tier, frame):
        place = {"frame": frame, "seq": its_tier}
        pl.semaphore_signal(semaphore, inc=1, device_id=place, device_id_type=MESH)

    @pl.when(jnp.logical_not(last))
    def _():
        def greet(step, carry):
            for frame in range(frames):
                signal(barrier, step + (step >= tier), frame)
            return carry

        lax.fori_loop(0, seqs - 1, greet, 0)
        for other in range(1, frames):
            signal(barrier, tier, lax.rem(my_frame + other, frames))

    small_copies = (
        pltpu.make_async_copy(slot_hbm, slot_ref, small_sems.at[0]),
        pltpu.make_async_copy(level_hbm, noise_ref, small_sems.at[1]),
    )

    def take_own(columns, size):
        for small_copy in small_copies:
            small_copy.start()
        lanes = pl.ds(0, size)
        both = (slice(None), pl.ds(columns.start, wide))
        pltpu.make_async_copy(gate_ref.at[both], gate_held, small_sems.at[2]).start()
        mine = (0, slice(None), slice(None), columns)
        held = (me, slice(None), slice(None), lanes)
        pltpu.make_async_copy(k_ref.at[mine], k_held.at[held], key_sem).start()
        pltpu.make_async_copy(v_ref.at[mine], v_held.at[held], value_sem).start()
        pltpu.make_async_copy(q_ref.at[mine], q_held.at[held], query_sems.at[tier]).start()

    pl.when(lower)(lambda: take_own(low_columns(tier, my_frame), narrow))
    pl.when(owns_wide)(lambda: take_own(high_columns(tier, my_frame), wide))

    pl.semaphore_wait(barrier, owning * frames - jnp.where(last, 0, 1))
    for stage_copy in stage_copies:
        stage_copy.wait()

    def arrived(held, semaphore):
        pltpu.make_async_copy(held, held, semaphore).wait()

    def push(source, target, send_sem, recv_sem, its_tier, frame):
        pltpu.make_async_remote_copy(
            src_ref=source,
            dst_ref=target,
            send_sem=send_sem,
            recv_sem=recv_sem,
            device_id={"frame": frame, "seq": its_tier},
            device_id_type=MESH,
        ).start()

    def blocks_for(high, its_tier, frame):
        columns = high_columns(its_tier, frame) if high else low_columns(its_tier, frame)
        lanes = pl.ds(0, wide if high else narrow)
        return (0, slice(None), slice(None), columns), (me, slice(None), slice(None), lanes)

    def send_keys(high, its_tier, frame):
        block, held = blocks_for(high, its_tier, frame)
        push(k_stage.at[block], k_held.at[held], send_sems.at[0], key_sem, its_tier, frame)
        push(v_stage.at[block], v_held.at[held], send_sems.at[1], value_sem, its_tier, frame)

    def send_queries(high, its_tier, frame):
        block, held = blocks_for(high, its_tier, frame)
        push(
            q_stage.at[block], q_held.at[held], send_sems.at[2], query_sems.at[tier], its_tier, frame
        )

    def to_low(send):
        for step in range(half):
            for frame in range(frames):
                send(False, jnp.int32(step), lax.rem(frame + my_frame, frames))

    def to_high(send):
        for step in range(quarter):
            for frame in range(frames):
                send(True, half + (step + lax.rem(tier, 2) * (1 - 2 * (step % 2))), lax.rem(frame + my_frame, frames))

    def beside(send, high, base, count):
        for step in range(count - 1):
            its_tier = base + step + (base + step >= tier)
            for frame in range(frames):
                send(high, its_tier, lax.rem(frame + my_frame, frames))
        for other in range(1, frames):
            send(high, tier, lax.rem(my_frame + other, frames))

    @pl.when(tier < quarter)
    def _():
        beside(send_keys, False, 0, half)
        to_high(send_keys)
        to_high(send_queries)
        beside(send_queries, False, 0, half)

    @pl.when(jnp.logical_and(tier >= quarter, lower))
    def _():
        to_high(send_keys)
        beside(send_keys, False, 0, half)
        beside(send_queries, False, 0, half)
        to_high(send_queries)

    @pl.when(owns_wide)
    def _():
        to_low(send_keys)
        beside(send_keys, True, half, quarter)
        to_low(send_queries)
        beside(send_queries, True, half, quarter)

    @pl.when(last)
    def _():
        to_high(send_keys)
        to_low(send_keys)
        to_low(send_queries)
        to_high(send_queries)


    @pl.when(last)
    def _():
        def announce(step, carry):
            for frame in range(frames):
                signal(ready_sem, step, frame)
            return carry

        lax.fori_loop(0, owning, announce, 0)

    def rows_of(block):
        return block.astype(jnp.float32).reshape(-1, HEAD).astype(jnp.bfloat16)

    factor = math.log2(math.e) / math.sqrt(HEAD)

    def serve(columns, size, order):
        for small_copy in small_copies:
            small_copy.wait()
        arrived(gate_held, small_sems.at[2])
        position = lax.broadcasted_iota(jnp.int32, (1, key_rows), 1)
        source = lax.div(position, rows_each)
        key_frame = lax.rem(source, frames) * local_frames + lax.rem(
            lax.div(position, tokens), local_frames
        )
        key_slot = jnp.zeros((1, key_rows), jnp.int32)
        for group in range(frames):
            for local in range(local_frames):
                key_slot = jnp.where(
                    key_frame == group * local_frames + local, slot_ref[group, local], key_slot
                )
        for group in range(frames):
            for local in range(local_frames):
                rows = pl.ds(local * tokens, tokens)
                bias[group, rows] = jnp.broadcast_to(
                    jnp.where(key_slot <= slot_ref[group, local], 0.0, MASKED), (tokens, key_rows)
                )
                gates[group, rows] = jnp.broadcast_to(
                    gate_held[pl.ds(noise_ref[group, local], 1), :], (tokens, wide)
                )

        lanes_of = [slice(start, start + HEAD) for start in range(0, size, HEAD)]
        held_lanes = pl.ds(0, size)
        pl.semaphore_wait(ready_sem, quarter * frames)
        arrived(k_held.at[:, :, :, held_lanes], key_sem)
        key_blocks = [rows_of(k_held[:, :, :, lanes]) for lanes in lanes_of]
        arrived(v_held.at[:, :, :, held_lanes], value_sem)
        value_blocks = [rows_of(v_held[:, :, :, lanes]) for lanes in lanes_of]
        target = out_ref.at[0, :, :, columns]

        def attend(first, count):
            for index in range(count):
                blocks = q_held.at[pl.ds((first + index) * frames, frames), :, :, held_lanes]
                arrived(blocks, query_sems.at[first + index])
            pieces = pl.ds(first * frames, count * frames)
            for lanes, key_block, value_block in zip(lanes_of, key_blocks, value_blocks):
                scores = lax.dot_general(
                    rows_of(q_held[pieces, :, :, lanes]),
                    key_block,
                    (((1,), (1,)), ((), ())),
                    preferred_element_type=jnp.float32,
                ).reshape(count, frames, rows_each, key_rows)
                seen = scores + bias[...][None]
                top = jnp.max(seen, axis=3, keepdims=True)
                weights = jnp.exp2((seen - top) * factor).astype(jnp.bfloat16).astype(jnp.float32)
                total = jnp.sum(weights, axis=3, keepdims=True)
                mixed = jnp.dot(
                    weights.reshape(-1, key_rows).astype(jnp.bfloat16),
                    value_block,
                    preferred_element_type=jnp.float32,
                ).reshape(count, frames, rows_each, HEAD)
                result = mixed / total * gates[:, :, lanes][None]
                answer[pieces, :, :, lanes] = result.reshape(
                    count * frames, local_frames, tokens, HEAD
                ).astype(jnp.bfloat16)

        def give_back(its_tier, frame):
            block = answer.at[its_tier * frames + frame, :, :, held_lanes]
            push(block, target, send_sems.at[3], out_sem, its_tier, frame)

        def reply(first, count):
            for step in range(count):
                for frame in range(frames):
                    give_back(jnp.int32(first + step), frame)

        def reply_beside(first, count):
            for step in range(count - 1):
                its_tier = first + step + (first + step >= tier)
                for frame in range(frames):
                    give_back(its_tier, frame)
            for other in range(1, frames):
                give_back(tier, lax.rem(my_frame + other, frames))
            block = answer.at[me, :, :, held_lanes]
            pltpu.make_async_copy(block, target, out_sem).start()

        for first, count, holds_me in order:
            attend(first, count)
            (reply_beside if holds_me else reply)(first, count)

    @pl.when(lower)
    def _():
        order = ((0, half, True), (owning, quarter, False), (half, quarter, False))
        serve(low_columns(tier, my_frame), narrow, order)

    @pl.when(owns_wide)
    def _():
        order = ((0, 1, False), (1, 1, False), (quarter, quarter, False), (half, half, True))
        serve(high_columns(tier, my_frame), wide, order)


    arrived(out_ref, out_sem)

    def sent(index, count, size):
        others = answer.at[pl.ds(0, count), :, :, pl.ds(0, size)]
        pltpu.make_async_copy(others, others, send_sems.at[index]).wait()

    def sent_inputs(count):
        for index in range(3):
            sent(index, count, narrow)

    @pl.when(lower)
    def _():
        sent_inputs(devices - 1)
        sent(3, devices - 1, narrow)

    @pl.when(owns_wide)
    def _():
        sent_inputs(devices - 2)
        sent(3, devices - 1, wide)

    pl.when(last)(lambda: sent_inputs(devices))


def uneven_call(plan, queries, keys, values, slot_of, level_of, gate_table):
    frames, seqs, heads_per = plan
    devices = frames * seqs
    _, local_frames, tokens, _ = queries.shape
    features = 2 * heads_per * HEAD
    block = (local_frames, tokens, features)
    rows = local_frames * tokens
    bf16 = jnp.bfloat16
    in_hbm = pl.BlockSpec(memory_space=pltpu.HBM)
    return pl.pallas_call(
        functools.partial(uneven_kernel, plan),
        out_shape=pltpu.VMEM(queries.shape, bf16),
        in_specs=[in_hbm] * 6,
        out_specs=pl.BlockSpec(memory_space=pl.ANY),
        scratch_shapes=[
            pltpu.SMEM(slot_of.shape, jnp.int32),
            pltpu.SMEM(level_of.shape, jnp.int32),
            pltpu.VMEM(queries.shape, bf16),
            pltpu.VMEM(queries.shape, bf16),
            pltpu.VMEM(queries.shape, bf16),
            pltpu.VMEM((devices,) + block, bf16),
            pltpu.VMEM((devices,) + block, bf16),
            pltpu.VMEM((devices,) + block, bf16),
            pltpu.VMEM((gate_table.shape[0], features), jnp.float32),
            pltpu.VMEM((frames, rows, devices * rows), jnp.float32),
            pltpu.VMEM((frames, rows, features), jnp.float32),
            pltpu.VMEM((devices,) + block, bf16),
            pltpu.SemaphoreType.DMA((6,)),
            pltpu.SemaphoreType.DMA((4,)),
            pltpu.SemaphoreType.DMA,
            pltpu.SemaphoreType.DMA,
            pltpu.SemaphoreType.DMA((seqs,)),
            pltpu.SemaphoreType.DMA,
            pltpu.SemaphoreType.REGULAR,
        ],
        compiler_params=pltpu.CompilerParams(collective_id=0, has_side_effects=True),
    )(slot_of, level_of, queries, keys, values, gate_table)


def solution(mesh):
    frames, seqs = mesh.shape["frame"], mesh.shape["seq"]
    devices = frames * seqs

    def body(queries, keys, values, slot_of, level_of, gate_table):
        _, local_frames, tokens, features = queries.shape
        heads = features // HEAD
        heads_per = max(1, heads // devices)
        copies = max(1, devices // heads)
        sources = devices // copies
        if seqs % 4 == 0 and heads % devices == 0:
            uneven_plan = (frames, seqs, heads // devices)
            return uneven_call(
                uneven_plan, queries, keys, values, slot_of, level_of, gate_table
            )
        tiers = math.gcd(8, seqs)
        pieces = math.gcd(8, seqs) if copies == 1 else 1
        fold = 0
        members = 2 if fold else 1
        plan = (frames, seqs, heads, heads_per, copies, sources, tiers, pieces, fold)
        block = (local_frames, tokens, HEAD)
        key_rows = devices * local_frames * tokens
        groups = frames if pieces > 1 else max(1, sources // seqs)
        per_piece = sources // pieces
        bf16 = jnp.bfloat16
        in_hbm = pl.BlockSpec(memory_space=pltpu.HBM)
        return pl.pallas_call(
            functools.partial(kernel, plan),
            out_shape=pltpu.VMEM(queries.shape, bf16),
            in_specs=[in_hbm] * 6,
            out_specs=pl.BlockSpec(memory_space=pl.ANY),
            scratch_shapes=[
                pltpu.SMEM(slot_of.shape, jnp.int32),
                pltpu.SMEM(level_of.shape, jnp.int32),
                pltpu.VMEM((heads,) + block, bf16),
                pltpu.VMEM((heads,) + block, bf16),
                pltpu.VMEM((heads,) + block, bf16),
                pltpu.VMEM((members, pieces, per_piece, heads_per) + block, bf16),
                pltpu.VMEM((members * devices, heads_per) + block, bf16),
                pltpu.VMEM((members * devices, heads_per) + block, bf16),
                pltpu.VMEM((members, gate_table.shape[0], heads_per * HEAD), jnp.float32),
                pltpu.VMEM((groups, local_frames * tokens, key_rows), jnp.float32),
                pltpu.VMEM(
                    (members, groups, local_frames * tokens, heads_per * HEAD), jnp.float32
                ),
                pltpu.VMEM(
                    (members, pieces, per_piece, local_frames, tokens, heads_per * HEAD), bf16
                ),
                pltpu.SemaphoreType.DMA((5 + members,)),
                pltpu.SemaphoreType.DMA((4,)),
                pltpu.SemaphoreType.DMA((members,)),
                pltpu.SemaphoreType.DMA((members,)),
                pltpu.SemaphoreType.DMA((members, pieces)),
                pltpu.SemaphoreType.DMA,
                pltpu.SemaphoreType.REGULAR((tiers,)),
            ],
            compiler_params=pltpu.CompilerParams(
                collective_id=0,
                has_side_effects=True,
            ),
        )(slot_of, level_of, queries, keys, values, gate_table)

    return jax.shard_map(
        body,
        mesh=mesh,
        in_specs=(
            P(("rollout", "frame"), None, "seq", None),
            P(("rollout", "frame"), None, "seq", None),
            P(("rollout", "frame"), None, "seq", None),
            P("rollout", None),
            P("rollout", None),
            P(),
        ),
        out_specs=P(("rollout", "frame"), None, "seq", None),
        check_vma=False,
    )
```
